32 devices in a mesh: level: 2 (over y), space: 4 (over z), col: 4 (over x, core).
Axes of the slice: x: 2, y: 2, z: 4, core: 2. Of those that a mesh axis runs over, the one named last changes fastest.
Arguments:
- emission: bfloat16 [512, 4096], P(('level', 'space', 'col')), parts along dimension 0, may hold values from 0.049804688 to 5
- reflect: float32 [32768], P(('level', 'space', 'col')), parts along dimension 0, may hold values from 0.2 to 0.9
- form_blocks: bfloat16 [512, 4, 4, 4096], P(('level', 'space'), 'col'), parts along dimension 0, may hold values from 0 to 0.03125
- block_rows: int32 [512, 4, 4], P(('level', 'space'), 'col'), parts along dimension 0, may hold values from 0 to 255, as said below
- view_grads: bfloat16 [8, 4, 4, 4, 4096], P(('level', 'space'), 'col'), parts along dimension 0, may hold values from -0.5 to 1.5
- view_rows: int32 [8, 4, 4, 4], P(('level', 'space'), 'col'), parts along dimension 0, may hold values from 0 to 63
- view_counts: int32 [8, 4, 4], P(('level', 'space'), 'col'), parts along dimension 0, may hold values from 1 to 4, as said below
Outputs:
- grad_emission: float32 [512, 4096], P(('level', 'space', 'col')), parts along dimension 0
- grad_reflect: float32 [32768], P(('level', 'space', 'col')), parts along dimension 0
The draws below stay inside these ranges and needn't reach their ends.
There are 2 independent parts, one for each index of `level`. The reference program is written for one: setup_inputs(seed, part) draws one part's arguments, and reference() takes and returns one part's arrays. A program takes and returns all parts, laid end to end along the dimension named above; each array names one. Nothing has to cross between parts.
Inputs may be any that keep to these rules, and one draw needn't show every extreme that they name: `block_rows`: the receiving block row of column block j lies in the same or an adjacent run of 64 blocks as j. `view_counts`: in every draw one owner receives 4 entries from every sender.
All inputs are finite; a program needn't handle non-finite values.
Results may differ from the reference program's by a relative error of at most 0.0003.
Values may be sent and summed in bfloat16 or wider, within the bound.
A program may use at most 128 MiB of HBM per device.

```python
import math
import jax
import jax.numpy as jnp
from jax import lax

BLK = 64
CONF = 64
BLOCKS_DEV = 64
SLOTS = 4
CAP = 4
NBLK = 256
PATCHES = 16384
N_SPACE = 4
N_COL = 4


def draw_form_blocks(key, part):
    top_value = 32.0 / (BLK * SLOTS * N_COL)
    entry = jnp.arange(BLK * BLK, dtype=jnp.int32)
    on_diagonal = entry // BLK == entry % BLK
    shape = (BLOCKS_DEV, N_COL, SLOTS, BLK * BLK)

    def draw_run(run_index):
        run_key = jax.random.fold_in(key, 1000 + run_index)
        kept = jax.random.randint(jax.random.fold_in(run_key, 31), shape, 0, 16, dtype=jnp.int32) == 0
        spread = jax.random.uniform(jax.random.fold_in(run_key, 32), shape, jnp.float32)
        diagonal_part = jax.random.uniform(jax.random.fold_in(run_key, 33), shape, jnp.float32, 0.25, 0.5)
        values = spread
        scattered = jnp.where(kept, values, 0.0)
        return (top_value * jnp.where(on_diagonal, diagonal_part, scattered)).astype(jnp.bfloat16)
    runs = lax.map(draw_run, jnp.arange(N_SPACE, dtype=jnp.int32))
    return runs.reshape(NBLK, N_COL, SLOTS, BLK * BLK)


def draw_block_rows(key, part):
    column = jnp.arange(NBLK, dtype=jnp.int32)[:, None, None]
    shard_index = column // BLOCKS_DEV
    lowest = jnp.maximum(shard_index - 1, 0) * BLOCKS_DEV
    highest = jnp.minimum(shard_index + 2, N_SPACE) * BLOCKS_DEV
    raw_bits = jax.random.randint(jax.random.fold_in(key, 11), (NBLK, N_COL, SLOTS), 0, 1 << 24, dtype=jnp.int32)
    return lowest + raw_bits % (highest - lowest)


def draw_view_counts(key, part):
    counts = jax.random.randint(jax.random.fold_in(key, 21), (N_SPACE, N_COL, N_SPACE), 1, CAP + 1, dtype=jnp.int32)
    busiest = jax.random.randint(jax.random.fold_in(key, 22), (), 0, N_SPACE, dtype=jnp.int32)
    owner = jnp.arange(N_SPACE, dtype=jnp.int32)[None, None, :]
    return jnp.where(owner == busiest, CAP, counts)


def set_ends(values, stream_key, smallest, largest):
    dims = values.shape
    index_at = [jax.random.randint(jax.random.fold_in(stream_key, axis), (), 0, dims[axis]) for axis in range(len(dims))]
    values = values.at[tuple(index_at)].set(smallest)
    longest = dims.index(max(dims))
    index_at[longest] = (index_at[longest] + 1) % dims[longest]
    return values.at[tuple(index_at)].set(largest)


def block_scale(stream_key, extent, shards, smallest, largest):
    def one(dim, shards_of):
        steps = jax.random.uniform(jax.random.fold_in(jax.random.fold_in(stream_key, 6), dim), (shards_of,), jnp.float32, smallest / len(shards), largest / len(shards))
        return jnp.repeat(jnp.exp(steps), extent[dim] // shards_of).reshape((-1,) + (1,) * (len(extent) - dim - 1))

    level = one(*shards[0])
    for cut in shards[1:]:
        level = level * one(*cut)
    return level


def setup_inputs(seed: int = 0, part: int = 0) -> dict:
    seeds = jax.random.split(jax.random.key(seed), 8)
    own_keys = jax.random.split(jax.random.fold_in(seeds[7], part), 8)
    return {
        "emission": jnp.clip(jnp.exp(math.log(5.0) - 4.609084 * jax.random.uniform(own_keys[0], (NBLK, BLK * CONF), jnp.float32) ** block_scale(own_keys[0], (NBLK, BLK * CONF), ((0, 16),), -0.2, 0.2)), 0.049804688, 5.0).astype(jnp.bfloat16),
        "reflect": jnp.clip(jnp.exp(math.log(0.9) - 1.50407736 * jax.random.uniform(own_keys[1], (PATCHES,), jnp.float32) ** block_scale(own_keys[1], (PATCHES,), ((0, 16),), -0.2, 0.2)), 0.2, 0.9),
        "form_blocks": draw_form_blocks(jax.random.fold_in(jax.random.fold_in(seeds[7], part), 71), part),
        "block_rows": draw_block_rows(jax.random.fold_in(jax.random.fold_in(seeds[7], part), 71), part),
        "view_grads": jnp.clip(-0.5 + 2.0 * jax.random.uniform(own_keys[4], (N_SPACE, N_COL, N_SPACE, CAP, BLK * CONF), jnp.float32) ** block_scale(own_keys[4], (N_SPACE, N_COL, N_SPACE, CAP, BLK * CONF), ((0, 4), (1, 4)), -0.2, 0.2), -0.5, 1.5).astype(jnp.bfloat16),
        "view_rows": set_ends(jax.random.randint(own_keys[5], (N_SPACE, N_COL, N_SPACE, CAP), 0, BLOCKS_DEV), jax.random.fold_in(own_keys[5], 1), 0, BLOCKS_DEV - 1).astype(jnp.int32),
        "view_counts": draw_view_counts(jax.random.fold_in(jax.random.fold_in(seeds[7], part), 71), part),
    }


def forward_all(form_blocks, block_rows, sources):
    def shard_step(running, step_index):
        start = (step_index * BLOCKS_DEV).astype(jnp.int32)
        blocks = lax.dynamic_slice_in_dim(form_blocks, start, BLOCKS_DEV, 0).astype(jnp.float32)
        blocks = blocks.reshape(BLOCKS_DEV, N_COL, SLOTS, BLK, BLK)
        column = lax.dynamic_slice_in_dim(sources, start, BLOCKS_DEV, 0).astype(jnp.float32)
        column = column.reshape(BLOCKS_DEV, BLK, CONF)
        block_terms = jnp.einsum("jckab,jbl->jckal", blocks, column)
        targets = lax.dynamic_slice_in_dim(block_rows, start, BLOCKS_DEV, 0).reshape(-1)
        return running.at[targets].add(block_terms.reshape(-1, BLK * CONF)), None

    initial = jnp.zeros((NBLK, BLK * CONF), jnp.float32)
    result, _ = lax.scan(shard_step, initial, jnp.arange(N_SPACE, dtype=jnp.int32))
    return result


def adjoint_all(form_blocks, block_rows, vector):
    def shard_step(carry, step_index):
        start = (step_index * BLOCKS_DEV).astype(jnp.int32)
        blocks = lax.dynamic_slice_in_dim(form_blocks, start, BLOCKS_DEV, 0).astype(jnp.float32)
        blocks = blocks.reshape(BLOCKS_DEV, N_COL, SLOTS, BLK, BLK)
        targets = lax.dynamic_slice_in_dim(block_rows, start, BLOCKS_DEV, 0).reshape(-1)
        picked = vector[targets].astype(jnp.float32).reshape(BLOCKS_DEV, N_COL, SLOTS, BLK, CONF)
        return carry, jnp.einsum("jckab,jckal->jbl", blocks, picked)

    _, pieces = lax.scan(shard_step, jnp.zeros((), jnp.float32), jnp.arange(N_SPACE, dtype=jnp.int32))
    return pieces.reshape(NBLK, BLK * CONF)


def reference(emission, reflect, form_blocks, block_rows, view_grads, view_rows, view_counts):
    gain = reflect.reshape(NBLK, BLK, 1)
    emitted = emission.astype(jnp.float32).reshape(NBLK, BLK, CONF)
    first_sums = forward_all(form_blocks, block_rows, emission)
    bounced = (emitted + gain * first_sums.reshape(NBLK, BLK, CONF)).reshape(NBLK, BLK * CONF).astype(jnp.bfloat16)
    second_sums = forward_all(form_blocks, block_rows, bounced)
    slot_index = lax.broadcasted_iota(jnp.int32, view_rows.shape, 3)
    owner = lax.broadcasted_iota(jnp.int32, view_rows.shape, 2)
    live_slots = slot_index < view_counts[..., None]
    targets = (owner * BLOCKS_DEV + view_rows).reshape(-1)
    slot_values = jnp.where(live_slots[..., None], view_grads.astype(jnp.float32), 0.0).reshape(-1, BLK * CONF)
    view_total = jnp.zeros((NBLK, BLK * CONF), jnp.float32).at[targets].add(slot_values)
    scaled_one = (gain * view_total.reshape(NBLK, BLK, CONF)).reshape(NBLK, BLK * CONF).astype(jnp.bfloat16)
    adjoint_one = adjoint_all(form_blocks, block_rows, scaled_one)
    scaled_two = (gain * adjoint_one.reshape(NBLK, BLK, CONF)).reshape(NBLK, BLK * CONF).astype(jnp.bfloat16)
    adjoint_two = adjoint_all(form_blocks, block_rows, scaled_two)
    grad_emission = view_total + adjoint_one + adjoint_two
    product = view_total * second_sums + adjoint_one * first_sums
    grad_reflect = product.reshape(NBLK, BLK, CONF).sum(axis=2).reshape(PATCHES)
    return grad_emission, grad_reflect
```

```python
import functools

import jax
import jax.numpy as jnp
from jax import lax
from jax.experimental import pallas as pl
from jax.experimental.pallas import tpu as pltpu
from jax.sharding import PartitionSpec as P

BLK = 64
CONF = 64
PK = BLK * CONF // 128
MESH = pl.DeviceIdType.MESH
F32 = jnp.float32
BF16 = jnp.bfloat16
VMEM_BYTES = 50 * 1024 * 1024


class Net:
    def __init__(self, send_sems, recv_sems):
        self.send_sems, self.recv_sems, self.used = send_sems, recv_sems, 0

    def copy(self, src, dst, target):
        n = self.used
        self.used += 1
        return pltpu.make_async_remote_copy(
            src_ref=src,
            dst_ref=dst,
            send_sem=self.send_sems.at[n],
            recv_sem=self.recv_sems.at[n],
            device_id=target,
            device_id_type=MESH,
        )


def place():
    col = lax.axis_index("col")
    return lax.axis_index("space"), col // 2, col % 2


def greet(n_x, z_all, n_s):
    s, x, core = place()
    barrier = pltpu.get_barrier_semaphore()
    targets = [{"col": 2 * x + 1 - core}]
    targets += [{"col": 2 * ((x + d) % n_x) + core} for d in range(1, n_x)]
    if z_all:
        targets += [{"space": (s + d) % n_s} for d in range(1, n_s)]
    for target in targets:
        pl.semaphore_signal(barrier, inc=1, device_id=target, device_id_type=MESH)
    if not z_all:

        @pl.when(s > 0)
        def _():
            pl.semaphore_signal(barrier, inc=1, device_id={"space": s - 1}, device_id_type=MESH)

        @pl.when(s < n_s - 1)
        def _():
            pl.semaphore_signal(barrier, inc=1, device_id={"space": s + 1}, device_id_type=MESH)

    if z_all:
        pl.semaphore_wait(barrier, len(targets))
    else:
        sides = (s > 0).astype(jnp.int32) + (s < n_s - 1).astype(jnp.int32)
        pl.semaphore_wait(barrier, len(targets) + sides)


def low_half(rows):
    return lax.broadcasted_iota(jnp.int32, (rows, 128), 1) < 64


class GatherCol:
    def __init__(self, net, buf, n_x, size, base=0):
        s, x, core = place()
        self.net, self.buf, self.n_x, self.size, self.base = net, buf, n_x, size, base
        self.x, self.core = x, core
        mine = self.piece(core, x)
        self.across = []
        for d in range(1, n_x):
            self.across.append(net.copy(mine, mine, {"col": 2 * ((x + d) % n_x) + core}))
        self.beside = [net.copy(mine, mine, {"col": 2 * x + 1 - core})]
        for cp in self.across + self.beside:
            cp.start()

    def piece(self, core, x):
        return self.buf.at[pl.ds(self.base + (core * self.n_x + x) * self.size, self.size)]

    def arrive_across(self):
        for d, cp in enumerate(self.across, 1):
            cp.wait_recv()
            got = self.piece(self.core, (self.x + self.n_x - d) % self.n_x)
            on = self.net.copy(got, got, {"col": 2 * self.x + 1 - self.core})
            on.start()
            self.beside.append(on)

    def finish(self):
        for cp in self.beside:
            cp.wait_recv()
        for cp in self.beside + self.across:
            cp.wait_send()


class GatherWindow:
    def __init__(self, net, buf, n_x, size, n_s):
        self.net, self.buf, self.n_s = net, buf, n_s
        self.run = 2 * n_x * size
        self.group = n_x * size
        self.col = GatherCol(net, buf, n_x, size, self.run)

    def half(self, run, core):
        return self.buf.at[pl.ds(run * self.run + core * self.group, self.group)]

    def along(self):
        s, x, core = place()
        n_s, net = self.n_s, self.net
        self.col.arrive_across()
        self.up = net.copy(self.half(1, core), self.half(0, core), {"space": s + 1})
        self.down = net.copy(self.half(1, core), self.half(2, core), {"space": s - 1})
        pl.when(s < n_s - 1)(self.up.start)
        pl.when(s > 0)(self.down.start)

    def finish(self):
        s, x, core = place()
        n_s, net = self.n_s, self.net
        other = {"col": 2 * x + 1 - core}
        before = net.copy(self.half(0, core), self.half(0, core), other)
        after = net.copy(self.half(2, core), self.half(2, core), other)

        @pl.when(s > 0)
        def _():
            self.up.wait_recv()
            before.start()

        @pl.when(s < n_s - 1)
        def _():
            self.down.wait_recv()
            after.start()

        self.col.finish()

        @pl.when(s > 0)
        def _():
            before.wait_recv()
            before.wait_send()
            self.down.wait_send()

        @pl.when(s < n_s - 1)
        def _():
            after.wait_recv()
            after.wait_send()
            self.up.wait_send()


class SumForward:
    def __init__(self, net, part, got_core, z_out, z_in, x_out, x_in, n_x, size, n_s):
        s, x, core = place()
        self.net, self.part, self.got_core = net, part, got_core
        self.z_out, self.z_in, self.x_out, self.x_in = z_out, z_in, x_out, x_in
        self.n_x, self.size, self.n_s = n_x, size, n_s
        self.run, self.group = 2 * n_x * size, n_x * size
        group = self.group
        self.first = []
        for r in (0, 2, 1):
            src = part.at[pl.ds(r * self.run + (1 - core) * group, group)]
            cp = net.copy(src, got_core.at[pl.ds(r * group, group)], {"col": 2 * x + 1 - core})
            cp.start()
            self.first.append(cp)

    def pair(self, r, start, count):
        s, x, core = place()
        mine = self.part[pl.ds(r * self.run + core * self.group + start, count)]
        return mine.astype(F32) + self.got_core[pl.ds(r * self.group + start, count)].astype(F32)

    def along(self):
        s, x, core = place()
        group = self.group
        self.z = [
            self.net.copy(self.z_out.at[0], self.z_in.at[1], {"space": s - 1}),
            self.net.copy(self.z_out.at[1], self.z_in.at[0], {"space": s + 1}),
        ]
        self.first[0].wait_recv()

        @pl.when(s > 0)
        def _():
            self.z_out[0] = self.pair(0, 0, group).astype(BF16)
            self.z[0].start()

        self.first[1].wait_recv()

        @pl.when(s < self.n_s - 1)
        def _():
            self.z_out[1] = self.pair(2, 0, group).astype(BF16)
            self.z[1].start()

        @pl.when(s == 0)
        def _():
            self.z_in[0] = jnp.zeros(self.z_in.shape[1:], BF16)

        @pl.when(s == self.n_s - 1)
        def _():
            self.z_in[1] = jnp.zeros(self.z_in.shape[1:], BF16)

    def rows(self, at):
        start, count = at * self.size, self.size
        total = self.pair(1, start, count)
        for side in range(2):
            total = total + self.z_in[side, pl.ds(start, count)].astype(F32)
        return total

    def across(self):
        s, x, core = place()
        self.first[2].wait_recv()
        pl.when(s > 0)(self.z[1].wait_recv)
        pl.when(s < self.n_s - 1)(self.z[0].wait_recv)
        self.x = []
        for d in range(1, self.n_x):
            to = (x + d) % self.n_x
            self.x_out[d - 1] = self.rows(to).astype(BF16)
            cp = self.net.copy(self.x_out.at[d - 1], self.x_in.at[d - 1], {"col": 2 * to + core})
            cp.start()
            self.x.append(cp)

    def finish(self):
        s, x, core = place()
        total = self.rows(x)
        for d in range(1, self.n_x):
            self.x[d - 1].wait_recv()
            total = total + self.x_in[d - 1].astype(F32)
        for cp in self.first + self.x:
            cp.wait_send()
        pl.when(s > 0)(self.z[0].wait_send)
        pl.when(s < self.n_s - 1)(self.z[1].wait_send)
        return total


class SumCol:
    def __init__(self, net, part, got_core, x_out, x_in, n_x, size):
        s, x, core = place()
        self.net, self.part, self.got_core = net, part, got_core
        self.x_out, self.x_in, self.n_x, self.size = x_out, x_in, n_x, size
        self.group = n_x * size
        self.first = []
        for d in list(range(1, n_x)) + [0]:
            to = (x + d) % n_x
            src = part.at[pl.ds((1 - core) * self.group + to * size, size)]
            cp = net.copy(src, got_core.at[pl.ds(to * size, size)], {"col": 2 * x + 1 - core})
            cp.start()
            self.first.append(cp)

    def rows(self, at):
        s, x, core = place()
        mine = self.part[pl.ds(core * self.group + at * self.size, self.size)]
        return mine + self.got_core[pl.ds(at * self.size, self.size)]

    def across(self):
        s, x, core = place()
        self.x = []
        for d in range(1, self.n_x):
            to = (x + d) % self.n_x
            self.first[d - 1].wait_recv()
            self.x_out[d - 1] = self.rows(to)
            cp = self.net.copy(self.x_out.at[d - 1], self.x_in.at[d - 1], {"col": 2 * to + core})
            cp.start()
            self.x.append(cp)

    def finish(self):
        s, x, core = place()
        self.first[-1].wait_recv()
        total = self.rows(x)
        for d in range(1, self.n_x):
            self.x[d - 1].wait_recv()
            total = total + self.x_in[d - 1]
        for cp in self.first + self.x:
            cp.wait_send()
        return total


def start_kernel(
    n_x, n_s, emission, view, meta, form, rows_perm, lanes_perm,
    src, views, metas, fwd_form, adj_form, unpacked, send_sems, recv_sems, local_sem,
):
    s, x, core = place()
    size = emission.shape[0]
    cap = view.shape[1]
    net = Net(send_sems, recv_sems)
    where = core * n_x + x
    for i in range(PK):
        unpacked[:, i, :] = emission[:, i * 128 : (i + 1) * 128].astype(F32)
    src[pl.ds(where * size, size)] = unpacked[...].astype(BF16)
    at = where * n_s + s
    own_view = pltpu.make_async_copy(view.at[s], views.at[at], local_sem.at[0])
    own_view.start()
    own_meta = pltpu.make_async_copy(meta.at[s], metas.at[at], local_sem.at[1])
    own_meta.start()
    greet(n_x, True, n_s)
    spread = []
    for d in range(1, n_s):
        to = (s + d) % n_s
        spread.append(net.copy(view.at[to], views.at[at], {"space": to}))
        spread.append(net.copy(meta.at[to], metas.at[at], {"space": to}))
    for cp in spread:
        cp.start()
    gather = GatherCol(net, src, n_x, size)

    def prepare(j, carry):
        c, r = j // size, j % size
        to = ((c % 2) * n_x + c // 2) * size + r
        plain = jnp.dot(rows_perm[...], form[j], preferred_element_type=F32).astype(BF16)
        fwd_form[to] = jnp.dot(plain, lanes_perm[...], preferred_element_type=F32).astype(BF16)
        adj_form[to] = lax.dot_general(
            lanes_perm[...], plain, (((0,), (1,)), ((), ())), preferred_element_type=F32
        ).astype(BF16)
        return carry

    half = form.shape[0] // 2
    lax.fori_loop(0, half, prepare, 0)
    own_view.wait()
    own_meta.wait()
    for cp in spread:
        cp.wait_recv()
    gather.arrive_across()
    more = [GatherCol(net, views, n_x, n_s), GatherCol(net, metas, n_x, n_s)]
    lax.fori_loop(half, form.shape[0], prepare, 0)
    for g in more:
        g.arrive_across()
    gather.finish()
    for g in more:
        g.finish()
    for cp in spread:
        cp.wait_send()


def forward_step(j, form, src, index, slots, window):
    low = low_half(PK)
    piece = src[j].astype(F32)
    turned = pltpu.roll(piece, 64, 1)
    zero = jnp.zeros_like(piece)
    wide = jnp.concatenate(
        [
            jnp.where(low, piece, zero),
            jnp.where(low, turned, zero),
            jnp.where(low, zero, turned),
            jnp.where(low, zero, piece),
        ],
        axis=0,
    ).astype(BF16)
    terms = jnp.dot(form[j], wide, preferred_element_type=F32)
    for k in range(slots):
        at = index[j * slots + k]
        window[at] = window[at] + terms[k * PK : (k + 1) * PK]


def adjoint_step(j, form, vector, index, slots, out):
    low = low_half(PK)
    picked = jnp.concatenate([vector[index[j * slots + k]] for k in range(slots)], axis=0)
    m = jnp.dot(form[j], picked, preferred_element_type=F32)
    even = m[:PK] + pltpu.roll(m[2 * PK : 3 * PK], 64, 1)
    odd = pltpu.roll(m[PK : 2 * PK], 64, 1) + m[3 * PK :]
    out[j] = jnp.where(low, even, odd)


def loop(count, step, unroll):
    def body(t, carry):
        for u in range(unroll):
            step(t * unroll + u)
        return carry

    lax.fori_loop(0, count // unroll, body, 0)


def clear(window):
    def body(t, carry):
        window[pl.ds(t * 8, 8)] = jnp.zeros((8,) + window.shape[1:], F32)
        return carry

    lax.fori_loop(0, window.shape[0] // 8, body, 0)


def write_part(window, part):
    def body(t, carry):
        part[pl.ds(t * 8, 8)] = window[pl.ds(t * 8, 8)].astype(BF16)
        return carry

    lax.fori_loop(0, window.shape[0] // 8, body, 0)


def first_local(slots, n_x, index, metas, form, src, views, gain, part, view_total, scaled, window, lists):
    c = lax.axis_index("col")
    size = view_total.shape[0]
    clear(window)
    loop(form.shape[0], lambda j: forward_step(j, form, src, index, slots, window), 4)
    write_part(window, part)
    view_total[...] = jnp.zeros_like(view_total)
    cap = views.shape[1]

    def one_list(t, carry):
        for i in range(PK):
            lists[:, i, :] = views[t, :, i * 128 : (i + 1) * 128].astype(F32)
        for q in range(cap):
            at = metas[t, 0, q] - c * size

            @pl.when((at >= 0) & (at < size))
            def _():
                view_total[at] = view_total[at] + lists[q]

        return carry

    lax.fori_loop(0, views.shape[0], one_list, 0)
    scaled[...] = (gain[...] * view_total[...]).astype(BF16)


def middle_kernel(
    n_x, n_s, part, src, gain, scaled, first_sums, bounced, vector,
    got_core, z_out, z_in, x_out, x_in, send_sems, recv_sems,
):
    s, x, core = place()
    size = scaled.shape[0]
    net = Net(send_sems, recv_sems)
    greet(n_x, False, n_s)
    mine = (core * n_x + x) * size
    run = 2 * n_x * size
    sums = SumForward(net, part, got_core, z_out, z_in, x_out, x_in, n_x, size, n_s)
    vector[pl.ds(run + mine, size)] = scaled[...]
    gather = GatherWindow(net, vector, n_x, size, n_s)
    sums.along()
    sums.across()
    gather.along()
    total = sums.finish()
    first_sums[...] = total
    bounced[pl.ds(mine, size)] = (src[pl.ds(mine, size)].astype(F32) + gain[...] * total).astype(BF16)
    second = GatherCol(net, bounced, n_x, size)
    second.arrive_across()
    gather.finish()
    second.finish()


def second_local(slots, index, fwd_form, adj_form, src, vector, part, adjoint, window):
    clear(window)

    def step(j):
        forward_step(j, fwd_form, src, index, slots, window)
        adjoint_step(j, adj_form, vector, index, slots, adjoint)

    loop(fwd_form.shape[0], step, 2)
    write_part(window, part)


def end_kernel(
    slots, n_x, n_s, index, part, adjoint, adj_form, first_sums, view_total, gain,
    grad_emission, grad_reflect,
    vector, last, keep, got_core, z_out, z_in, x_out, x_in,
    one_core, one_out, one_in, two_core, two_out, two_in, send_sems, recv_sems,
):
    s, x, core = place()
    size = view_total.shape[0]
    net = Net(send_sems, recv_sems)
    greet(n_x, False, n_s)
    mine = (core * n_x + x) * size
    run = 2 * n_x * size
    one = SumCol(net, adjoint, one_core, one_out, one_in, n_x, size)
    one.across()
    sums = SumForward(net, part, got_core, z_out, z_in, x_out, x_in, n_x, size, n_s)
    sums.along()
    adjoint_one = one.finish()
    vector[pl.ds(run + mine, size)] = (gain[...] * adjoint_one).astype(BF16)
    keep[...] = adjoint_one
    gather = GatherWindow(net, vector, n_x, size, n_s)
    gather.along()
    sums.across()
    gather.finish()
    loop(adj_form.shape[0], lambda j: adjoint_step(j, adj_form, vector, index, slots, last), 4)
    two = SumCol(net, last, two_core, two_out, two_in, n_x, size)
    two.across()
    second_sums = sums.finish()
    product = view_total[...] * second_sums + keep[...] * first_sums[...]
    low = lax.broadcasted_iota(jnp.int32, product.shape, 2) < 64
    grad_reflect[0] = jnp.sum(jnp.where(low, product, 0.0), axis=2)
    grad_reflect[1] = jnp.sum(jnp.where(low, 0.0, product), axis=2)
    keep[...] = view_total[...] + keep[...] + two.finish()
    for i in range(PK):
        grad_emission[:, i * 128 : (i + 1) * 128] = keep[:, i, :]


def call(kernel, outs, scratch, operands, smem=0, remote=None):
    vmem = pl.BlockSpec(memory_space=pltpu.VMEM)
    specs = [pl.BlockSpec(memory_space=pltpu.SMEM)] * smem + [vmem] * (len(operands) - smem)
    if remote is None:
        params = pltpu.CompilerParams(vmem_limit_bytes=VMEM_BYTES)
    else:
        params = pltpu.CompilerParams(
            vmem_limit_bytes=VMEM_BYTES, collective_id=remote, has_side_effects=True
        )
    return pl.pallas_call(
        kernel,
        out_shape=[jax.ShapeDtypeStruct(*out) for out in outs],
        in_specs=specs,
        out_specs=[vmem] * len(outs),
        scratch_shapes=scratch,
        compiler_params=params,
    )(*operands)


def body(n_s, n_c, emission, reflect, form_blocks, block_rows, view_grads, view_rows, view_counts):
    n_x = n_c // 2
    rows, slots = form_blocks.shape[0], form_blocks.shape[2]
    size = emission.shape[0]
    cap = view_grads.shape[3]
    s = lax.axis_index("space")
    tall = slots * PK
    form = form_blocks.reshape(rows, slots, PK, 128).transpose(0, 2, 1, 3).reshape(rows, tall, 128)
    a, b = jnp.arange(tall)[:, None], jnp.arange(tall)[None, :]
    rows_perm = ((a % PK) * slots + a // PK == b).astype(BF16)
    q, p = jnp.arange(128)[:, None], jnp.arange(128)[None, :]
    lanes_perm = (q == (p // 64) * 64 + 2 * (p % 32) + (p % 64) // 32).astype(BF16)
    target = block_rows.reshape(rows, slots) - (s - 1) * rows
    block = target % rows
    piece = block // size
    target = target - block + ((piece % 2) * n_x + piece // 2) * size + block % size
    index = target.reshape(n_x, 2, size, slots).transpose(1, 0, 2, 3).reshape(rows * slots)
    live = jnp.arange(cap, dtype=jnp.int32) < view_counts[0, 0][:, None]
    meta = jnp.where(live, view_rows[0, 0], -1)
    meta = jnp.pad(meta, ((0, 0), (0, 128 - cap)))[:, None, :]
    gain = jnp.broadcast_to(reflect.reshape(size, PK, 2, 1), (size, PK, 2, 64)).reshape(size, PK, 128)

    dma = pltpu.SemaphoreType.DMA
    blocks = lambda n: (n, PK, 128)
    src, views, metas, fwd_form, adj_form = call(
        functools.partial(start_kernel, n_x, n_s),
        [
            (blocks(rows), BF16),
            ((n_c * n_s, cap, BLK * CONF), BF16),
            ((n_c * n_s, 1, 128), jnp.int32),
            ((rows, tall, 128), BF16),
            ((rows, 128, tall), BF16),
        ],
        [pltpu.VMEM(blocks(size), F32)] + [dma((2 * n_s + 6 * n_x,))] * 2 + [dma((2,))],
        (emission, view_grads[0, 0], meta, form, rows_perm, lanes_perm),
        remote=0,
    )
    part_one, view_total, scaled_one = call(
        functools.partial(first_local, slots, n_x),
        [(blocks(3 * rows), BF16), (blocks(size), F32), (blocks(size), BF16)],
        [pltpu.VMEM(blocks(3 * rows), F32), pltpu.VMEM(blocks(cap), F32)],
        (index, metas, fwd_form, src, views, gain),
        smem=2,
    )
    group = n_x * size
    sum_bufs = [
        pltpu.VMEM(blocks(3 * group), BF16),
        pltpu.VMEM((2,) + blocks(group), BF16),
        pltpu.VMEM((2,) + blocks(group), BF16),
        pltpu.VMEM((n_x - 1,) + blocks(size), BF16),
        pltpu.VMEM((n_x - 1,) + blocks(size), BF16),
    ]
    first_sums, bounced, vector = call(
        functools.partial(middle_kernel, n_x, n_s),
        [(blocks(size), F32), (blocks(rows), BF16), (blocks(3 * rows), BF16)],
        sum_bufs + [dma((9 + 5 * n_x,))] * 2,
        (part_one, src, gain, scaled_one),
        remote=1,
    )
    part_two, adjoint_one = call(
        functools.partial(second_local, slots),
        [(blocks(3 * rows), BF16), (blocks(rows), F32)],
        [pltpu.VMEM(blocks(3 * rows), F32)],
        (index, fwd_form, adj_form, bounced, vector),
        smem=1,
    )
    col_bufs = [
        pltpu.VMEM(blocks(group), F32),
        pltpu.VMEM((n_x - 1,) + blocks(size), F32),
        pltpu.VMEM((n_x - 1,) + blocks(size), F32),
    ]
    grad_emission, grad_reflect = call(
        functools.partial(end_kernel, slots, n_x, n_s),
        [((size, BLK * CONF), F32), ((2, size, PK), F32)],
        [pltpu.VMEM(blocks(3 * rows), BF16), pltpu.VMEM(blocks(rows), F32), pltpu.VMEM(blocks(size), F32)]
        + sum_bufs + col_bufs * 2 + [dma((9 + 8 * n_x,))] * 2,
        (index, part_two, adjoint_one, adj_form, first_sums, view_total, gain),
        smem=1,
        remote=2,
    )
    return grad_emission, grad_reflect.transpose(1, 2, 0).reshape(size * BLK)


def solution(mesh):
    in_specs = (
        P(("level", "space", "col"), None),
        P(("level", "space", "col")),
        P(("level", "space"), "col", None, None),
        P(("level", "space"), "col", None),
        P(("level", "space"), "col", None, None, None),
        P(("level", "space"), "col", None, None),
        P(("level", "space"), "col", None),
    )
    out_specs = (P(("level", "space", "col"), None), P(("level", "space", "col")))
    step = functools.partial(body, mesh.shape["space"], mesh.shape["col"])
    return jax.shard_map(step, mesh=mesh, in_specs=in_specs, out_specs=out_specs, check_vma=False)
```

```python
import functools

import jax
import jax.numpy as jnp
from jax import lax
from jax.experimental import pallas as pl
from jax.experimental.pallas import tpu as pltpu
from jax.sharding import PartitionSpec as P

BLK = 64
CONF = 64
PK = BLK * CONF // 128
MESH = pl.DeviceIdType.MESH
F32 = jnp.float32
BF16 = jnp.bfloat16
VMEM_BYTES = 32 * 1024 * 1024


class Net:
    def __init__(self, send_sems, recv_sems):
        self.send_sems, self.recv_sems, self.used = send_sems, recv_sems, 0

    def copy(self, src, dst, target):
        n = self.used
        self.used += 1
        return pltpu.make_async_remote_copy(
            src_ref=src,
            dst_ref=dst,
            send_sem=self.send_sems.at[n],
            recv_sem=self.recv_sems.at[n],
            device_id=target,
            device_id_type=MESH,
        )


def place():
    col = lax.axis_index("col")
    return lax.axis_index("space"), col // 2, col % 2


def greet(n_x, z_all, n_s):
    s, x, core = place()
    barrier = pltpu.get_barrier_semaphore()
    targets = [{"col": 2 * x + 1 - core}]
    targets += [{"col": 2 * ((x + d) % n_x) + core} for d in range(1, n_x)]
    if z_all:
        targets += [{"space": (s + d) % n_s} for d in range(1, n_s)]
    for target in targets:
        pl.semaphore_signal(barrier, inc=1, device_id=target, device_id_type=MESH)
    if not z_all:

        @pl.when(s > 0)
        def _():
            pl.semaphore_signal(barrier, inc=1, device_id={"space": s - 1}, device_id_type=MESH)

        @pl.when(s < n_s - 1)
        def _():
            pl.semaphore_signal(barrier, inc=1, device_id={"space": s + 1}, device_id_type=MESH)

    if z_all:
        pl.semaphore_wait(barrier, len(targets))
    else:
        sides = (s > 0).astype(jnp.int32) + (s < n_s - 1).astype(jnp.int32)
        pl.semaphore_wait(barrier, len(targets) + sides)


def low_half(rows):
    return lax.broadcasted_iota(jnp.int32, (rows, 128), 1) < 64


class GatherCol:
    def __init__(self, net, buf, n_x, size, base=0):
        s, x, core = place()
        self.net, self.buf, self.n_x, self.size, self.base = net, buf, n_x, size, base
        self.x, self.core = x, core
        mine = self.piece(core, x)
        self.across = []
        for d in range(1, n_x):
            self.across.append(net.copy(mine, mine, {"col": 2 * ((x + d) % n_x) + core}))
        self.beside = [net.copy(mine, mine, {"col": 2 * x + 1 - core})]
        for cp in self.across + self.beside:
            cp.start()

    def piece(self, core, x):
        return self.buf.at[pl.ds(self.base + (core * self.n_x + x) * self.size, self.size)]

    def arrive_across(self):
        for d, cp in enumerate(self.across, 1):
            cp.wait_recv()
            got = self.piece(self.core, (self.x + self.n_x - d) % self.n_x)
            on = self.net.copy(got, got, {"col": 2 * self.x + 1 - self.core})
            on.start()
            self.beside.append(on)

    def finish(self):
        for cp in self.beside:
            cp.wait_recv()
        for cp in self.beside + self.across:
            cp.wait_send()


class GatherWindow:
    def __init__(self, net, buf, n_x, size, n_s):
        self.net, self.buf, self.n_s = net, buf, n_s
        self.run = 2 * n_x * size
        self.group = n_x * size
        self.col = GatherCol(net, buf, n_x, size, self.run)

    def half(self, run, core):
        return self.buf.at[pl.ds(run * self.run + core * self.group, self.group)]

    def along(self):
        s, x, core = place()
        n_s, net = self.n_s, self.net
        self.col.arrive_across()
        self.up = net.copy(self.half(1, core), self.half(0, core), {"space": s + 1})
        self.down = net.copy(self.half(1, core), self.half(2, core), {"space": s - 1})
        pl.when(s < n_s - 1)(self.up.start)
        pl.when(s > 0)(self.down.start)

    def finish(self):
        s, x, core = place()
        n_s, net = self.n_s, self.net
        other = {"col": 2 * x + 1 - core}
        before = net.copy(self.half(0, core), self.half(0, core), other)
        after = net.copy(self.half(2, core), self.half(2, core), other)

        @pl.when(s > 0)
        def _():
            self.up.wait_recv()
            before.start()

        @pl.when(s < n_s - 1)
        def _():
            self.down.wait_recv()
            after.start()

        self.col.finish()

        @pl.when(s > 0)
        def _():
            before.wait_recv()
            before.wait_send()
            self.down.wait_send()

        @pl.when(s < n_s - 1)
        def _():
            after.wait_recv()
            after.wait_send()
            self.up.wait_send()


class SumForward:
    def __init__(self, net, part, got_core, z_out, z_in, x_out, x_in, n_x, size, n_s):
        s, x, core = place()
        self.net, self.part, self.got_core = net, part, got_core
        self.z_out, self.z_in, self.x_out, self.x_in = z_out, z_in, x_out, x_in
        self.n_x, self.size, self.n_s = n_x, size, n_s
        self.run, self.group = 2 * n_x * size, n_x * size
        group = self.group
        self.first = []
        for r in (0, 2, 1):
            src = part.at[pl.ds(r * self.run + (1 - core) * group, group)]
            cp = net.copy(src, got_core.at[pl.ds(r * group, group)], {"col": 2 * x + 1 - core})
            cp.start()
            self.first.append(cp)

    def pair(self, r, start, count):
        s, x, core = place()
        mine = self.part[pl.ds(r * self.run + core * self.group + start, count)]
        return mine.astype(F32) + self.got_core[pl.ds(r * self.group + start, count)].astype(F32)

    def along(self):
        s, x, core = place()
        group = self.group
        self.z = [
            self.net.copy(self.z_out.at[0], self.z_in.at[1], {"space": s - 1}),
            self.net.copy(self.z_out.at[1], self.z_in.at[0], {"space": s + 1}),
        ]
        self.first[0].wait_recv()

        @pl.when(s > 0)
        def _():
            self.z_out[0] = self.pair(0, 0, group).astype(BF16)
            self.z[0].start()

        self.first[1].wait_recv()

        @pl.when(s < self.n_s - 1)
        def _():
            self.z_out[1] = self.pair(2, 0, group).astype(BF16)
            self.z[1].start()

        @pl.when(s == 0)
        def _():
            self.z_in[0] = jnp.zeros(self.z_in.shape[1:], BF16)

        @pl.when(s == self.n_s - 1)
        def _():
            self.z_in[1] = jnp.zeros(self.z_in.shape[1:], BF16)

    def rows(self, at):
        start, count = at * self.size, self.size
        total = self.pair(1, start, count)
        for side in range(2):
            total = total + self.z_in[side, pl.ds(start, count)].astype(F32)
        return total

    def across(self):
        s, x, core = place()
        self.first[2].wait_recv()
        pl.when(s > 0)(self.z[1].wait_recv)
        pl.when(s < self.n_s - 1)(self.z[0].wait_recv)
        self.x = []
        for d in range(1, self.n_x):
            to = (x + d) % self.n_x
            self.x_out[d - 1] = self.rows(to)
            cp = self.net.copy(self.x_out.at[d - 1], self.x_in.at[d - 1], {"col": 2 * to + core})
            cp.start()
            self.x.append(cp)

    def finish(self):
        s, x, core = place()
        total = self.rows(x)
        for d in range(1, self.n_x):
            self.x[d - 1].wait_recv()
            total = total + self.x_in[d - 1]
        for cp in self.first + self.x:
            cp.wait_send()
        pl.when(s > 0)(self.z[0].wait_send)
        pl.when(s < self.n_s - 1)(self.z[1].wait_send)
        return total


class SumCol:
    def __init__(self, net, part, got_core, x_out, x_in, n_x, size):
        s, x, core = place()
        self.net, self.part, self.got_core = net, part, got_core
        self.x_out, self.x_in, self.n_x, self.size = x_out, x_in, n_x, size
        self.group = n_x * size
        self.first = []
        for d in list(range(1, n_x)) + [0]:
            to = (x + d) % n_x
            src = part.at[pl.ds((1 - core) * self.group + to * size, size)]
            cp = net.copy(src, got_core.at[pl.ds(to * size, size)], {"col": 2 * x + 1 - core})
            cp.start()
            self.first.append(cp)

    def rows(self, at):
        s, x, core = place()
        mine = self.part[pl.ds(core * self.group + at * self.size, self.size)]
        return mine + self.got_core[pl.ds(at * self.size, self.size)]

    def across(self):
        s, x, core = place()
        self.x = []
        for d in range(1, self.n_x):
            to = (x + d) % self.n_x
            self.first[d - 1].wait_recv()
            self.x_out[d - 1] = self.rows(to)
            cp = self.net.copy(self.x_out.at[d - 1], self.x_in.at[d - 1], {"col": 2 * to + core})
            cp.start()
            self.x.append(cp)

    def finish(self):
        s, x, core = place()
        self.first[-1].wait_recv()
        total = self.rows(x)
        for d in range(1, self.n_x):
            self.x[d - 1].wait_recv()
            total = total + self.x_in[d - 1]
        for cp in self.first + self.x:
            cp.wait_send()
        return total


def patch_masks(p):
    i = lax.broadcasted_iota(jnp.int32, (PK, 128), 0)
    t = lax.broadcasted_iota(jnp.int32, (PK, 128), 1)
    rows = t == (p % 2) * 64 + 2 * i + t % 2
    patch = lax.broadcasted_iota(jnp.int32, (128, 128), 0)
    lane = lax.broadcasted_iota(jnp.int32, (128, 128), 1)
    return rows, (patch % 2 == lane // 64).astype(F32)


def start_kernel(
    n_x, n_s, emission, reflect, view, meta, form, rows_perm, lanes_perm,
    src, fwd_form, adj_form, gain, view_total, vector,
    views, metas, entries, unpacked, send_sems, recv_sems, local_sem,
):
    s, x, core = place()
    size = emission.shape[0]
    cap = view.shape[1]
    rows = form.shape[0]
    net = Net(send_sems, recv_sems)
    where = core * n_x + x
    for i in range(PK):
        unpacked[:, i, :] = emission[:, i * 128 : (i + 1) * 128].astype(F32)
    src[pl.ds(where * size, size)] = unpacked[...].astype(BF16)
    at = where * n_s + s
    own_view = pltpu.make_async_copy(view.at[s], views.at[at], local_sem.at[0])
    own_view.start()
    own_meta = pltpu.make_async_copy(meta.at[s], metas.at[at], local_sem.at[1])
    own_meta.start()
    greet(n_x, True, n_s)
    spread = []
    for d in range(1, n_s):
        to = (s + d) % n_s
        spread.append(net.copy(view.at[to], views.at[at], {"space": to}))
        spread.append(net.copy(meta.at[to], metas.at[at], {"space": to}))
    for cp in spread:
        cp.start()
    gather = GatherCol(net, src, n_x, size)

    def prepare(j):
        c, r = j // size, j % size
        to = ((c % 2) * n_x + c // 2) * size + r
        plain = jnp.dot(rows_perm[...], form[j], preferred_element_type=F32).astype(BF16)
        fwd_form[to] = jnp.dot(plain, lanes_perm[...], preferred_element_type=F32).astype(BF16)
        adj_form[to] = lax.dot_general(
            lanes_perm[...], plain, (((0,), (1,)), ((), ())), preferred_element_type=F32
        ).astype(BF16)

    loop(0, rows // 4, prepare, 8)
    for p in range(size):
        sel, lanes = patch_masks(p)
        picked = jnp.where(sel, reflect[p // 2 : p // 2 + 1, :], 0.0)
        gain[p] = jnp.dot(
            picked, lanes, preferred_element_type=F32, precision=lax.Precision.HIGHEST
        )
    own_view.wait()
    own_meta.wait()
    for cp in spread:
        cp.wait_recv()
    more = [GatherCol(net, views, n_x, n_s), GatherCol(net, metas, n_x, n_s)]
    gather.arrive_across()
    loop(rows // 4, rows // 4, prepare, 8)
    for g in more:
        g.arrive_across()
    gather.finish()
    for g in more:
        g.finish()
    count = views.shape[0] * cap
    for t in range(views.shape[0]):
        entries[t * cap : (t + 1) * cap, :] = views[t].astype(F32)
    marks = jnp.sum(metas[...], axis=0)
    wanted = lax.broadcasted_iota(jnp.int32, (size, marks.shape[1]), 0) + (2 * x + core) * size + 1
    chosen = (wanted == marks).astype(F32).astype(BF16)[:, :count]
    for i in range(0, PK, 4):
        cut = entries[:, i * 128 : (i + 4) * 128].astype(BF16)
        found = jnp.dot(chosen, cut, preferred_element_type=F32)
        for u in range(4):
            view_total[:, i + u, :] = found[:, u * 128 : (u + 1) * 128]
    vector[pl.ds(2 * n_x * size + where * size, size)] = (gain[...] * view_total[...]).astype(BF16)
    window = GatherWindow(net, vector, n_x, size, n_s)
    loop(rows // 2, rows // 4, prepare, 8)
    window.along()
    loop(rows // 2 + rows // 4, rows // 4, prepare, 8)
    window.finish()
    for cp in spread:
        cp.wait_send()


def forward_step(j, form, src, index, slots, window):
    low = low_half(PK)
    piece = src[j].astype(F32)
    turned = pltpu.roll(piece, 64, 1)
    zero = jnp.zeros_like(piece)
    wide = jnp.concatenate(
        [
            jnp.where(low, piece, zero),
            jnp.where(low, turned, zero),
            jnp.where(low, zero, turned),
            jnp.where(low, zero, piece),
        ],
        axis=0,
    ).astype(BF16)
    terms = jnp.dot(form[j], wide, preferred_element_type=F32)
    for k in range(slots):
        at = index[j * slots + k]
        window[at] = window[at] + terms[k * PK : (k + 1) * PK]


def adjoint_step(j, form, vector, index, slots, out):
    low = low_half(PK)
    picked = jnp.concatenate([vector[index[j * slots + k]] for k in range(slots)], axis=0)
    m = jnp.dot(form[j], picked, preferred_element_type=F32)
    even = m[:PK] + pltpu.roll(m[2 * PK : 3 * PK], 64, 1)
    odd = pltpu.roll(m[PK : 2 * PK], 64, 1) + m[3 * PK :]
    out[j] = jnp.where(low, even, odd)


def loop(first, count, step, unroll):
    def body(t, carry):
        for u in range(unroll):
            step(first + t * unroll + u)
        return carry

    lax.fori_loop(0, count // unroll, body, 0)


def clear(window):
    def body(t, carry):
        window[pl.ds(t * 8, 8)] = jnp.zeros((8,) + window.shape[1:], F32)
        return carry

    lax.fori_loop(0, window.shape[0] // 8, body, 0)


def write_part(window, part):
    def body(t, carry):
        part[pl.ds(t * 8, 8)] = window[pl.ds(t * 8, 8)].astype(BF16)
        return carry

    lax.fori_loop(0, window.shape[0] // 8, body, 0)


def forward_local(slots, index, form, src, part, window):
    clear(window)
    loop(0, form.shape[0], lambda j: forward_step(j, form, src, index, slots, window), 8)
    write_part(window, part)


def middle_kernel(
    slots, n_x, n_s, index, part, src, gain, vector, adj_form,
    first_sums, bounced, adjoint_one, next_vector,
    got_core, z_out, z_in, x_out, x_in,
    terms, one_core, one_out, one_in, send_sems, recv_sems,
):
    s, x, core = place()
    size = gain.shape[0]
    net = Net(send_sems, recv_sems)
    greet(n_x, False, n_s)
    mine = (core * n_x + x) * size
    group = n_x * size
    step = lambda j: adjoint_step(j, adj_form, vector, index, slots, terms)
    sums = SumForward(net, part, got_core, z_out, z_in, x_out, x_in, n_x, size, n_s)
    loop((1 - core) * group, group, step, 8)
    one = SumCol(net, terms, one_core, one_out, one_in, n_x, size)
    sums.along()
    loop(core * group, group, step, 8)
    one.across()
    sums.across()
    adjoint_one[...] = one.finish()
    next_vector[pl.ds(2 * group + mine, size)] = (gain[...] * adjoint_one[...]).astype(BF16)
    gather = GatherWindow(net, next_vector, n_x, size, n_s)
    first_sums[...] = sums.finish()
    bounced[pl.ds(mine, size)] = (
        src[pl.ds(mine, size)].astype(F32) + gain[...] * first_sums[...]
    ).astype(BF16)
    second = GatherCol(net, bounced, n_x, size)
    gather.along()
    second.arrive_across()
    gather.finish()
    second.finish()


def end_kernel(
    slots, n_x, n_s, index, part, vector, adj_form, first_sums, adjoint_one, view_total,
    grad_emission, grad_reflect,
    got_core, z_out, z_in, x_out, x_in,
    terms, two_core, two_out, two_in, send_sems, recv_sems,
):
    s, x, core = place()
    size = view_total.shape[0]
    net = Net(send_sems, recv_sems)
    greet(n_x, False, n_s)
    group = n_x * size
    step = lambda j: adjoint_step(j, adj_form, vector, index, slots, terms)
    sums = SumForward(net, part, got_core, z_out, z_in, x_out, x_in, n_x, size, n_s)
    loop((1 - core) * group, group, step, 8)
    two = SumCol(net, terms, two_core, two_out, two_in, n_x, size)
    sums.along()
    loop(core * group, group, step, 8)
    two.across()
    sums.across()
    got_two = two.finish()
    keep = two_core
    keep[pl.ds(0, size)] = view_total[...] + adjoint_one[...] + got_two
    for i in range(PK):
        grad_emission[:, i * 128 : (i + 1) * 128] = keep[:size, i, :]
    keep[pl.ds(0, size)] = view_total[...] * sums.finish() + adjoint_one[...] * first_sums[...]
    for p in range(0, size, 2):
        total = jnp.zeros((1, 128), F32)
        for q in (p, p + 1):
            sel, lanes = patch_masks(q)
            spread = lax.dot_general(
                keep[q], lanes, (((1,), (1,)), ((), ())),
                preferred_element_type=F32, precision=lax.Precision.HIGHEST,
            )
            total = total + jnp.sum(jnp.where(sel, spread, 0.0), axis=0, keepdims=True)
        grad_reflect[p // 2 : p // 2 + 1, :] = total


def call(kernel, outs, scratch, operands, smem=0, remote=None):
    vmem = pl.BlockSpec(memory_space=pltpu.VMEM)
    specs = [pl.BlockSpec(memory_space=pltpu.SMEM)] * smem + [vmem] * (len(operands) - smem)
    if remote is None:
        params = pltpu.CompilerParams(vmem_limit_bytes=VMEM_BYTES)
    else:
        params = pltpu.CompilerParams(
            vmem_limit_bytes=VMEM_BYTES, collective_id=remote, has_side_effects=True
        )
    return pl.pallas_call(
        kernel,
        out_shape=[jax.ShapeDtypeStruct(*out) for out in outs],
        in_specs=specs,
        out_specs=[vmem] * len(outs),
        scratch_shapes=scratch,
        compiler_params=params,
    )(*operands)


def body(n_s, n_c, emission, reflect, form_blocks, block_rows, view_grads, view_rows, view_counts):
    n_x = n_c // 2
    rows, slots = form_blocks.shape[0], form_blocks.shape[2]
    size = emission.shape[0]
    cap = view_grads.shape[3]
    s = lax.axis_index("space")
    tall = slots * PK
    form = form_blocks.reshape(rows, slots, PK, 128).transpose(0, 2, 1, 3).reshape(rows, tall, 128)
    a, b = jnp.arange(tall)[:, None], jnp.arange(tall)[None, :]
    rows_perm = ((a % PK) * slots + a // PK == b).astype(BF16)
    q, p = jnp.arange(128)[:, None], jnp.arange(128)[None, :]
    lanes_perm = (q == (p // 64) * 64 + 2 * (p % 32) + (p % 64) // 32).astype(BF16)
    target = block_rows.reshape(rows, slots) - (s - 1) * rows
    block = target % rows
    piece = block // size
    target = target - block + ((piece % 2) * n_x + piece // 2) * size + block % size
    index = target.reshape(n_x, 2, size, slots).transpose(1, 0, 2, 3).reshape(rows * slots)
    col = lax.axis_index("col")
    lists = n_c * n_s
    at = ((col % 2) * n_x + col // 2) * n_s + s
    live = jnp.arange(cap, dtype=jnp.int32) < view_counts[0, 0][:, None]
    marks = jnp.where(live, view_rows[0, 0] + 1, 0)[:, None, :]
    own_list = jnp.arange(lists, dtype=jnp.int32)[None, :, None] == at
    meta = jnp.where(own_list, marks, 0).reshape(n_s, lists * cap)
    meta = jnp.pad(meta, ((0, 0), (0, -(lists * cap) % 128)))[:, None, :]

    dma = pltpu.SemaphoreType.DMA
    blocks = lambda n: (n, PK, 128)
    src, fwd_form, adj_form, gain, view_total, vector = call(
        functools.partial(start_kernel, n_x, n_s),
        [
            (blocks(rows), BF16),
            ((rows, tall, 128), BF16),
            ((rows, 128, tall), BF16),
            (blocks(size), F32),
            (blocks(size), F32),
            (blocks(3 * rows), BF16),
        ],
        [
            pltpu.VMEM((lists, cap, BLK * CONF), BF16),
            pltpu.VMEM((lists,) + meta.shape[1:], jnp.int32),
            pltpu.VMEM((lists * cap, BLK * CONF), F32),
            pltpu.VMEM(blocks(size), F32),
        ]
        + [dma((4 + 2 * n_s + 8 * n_x,))] * 2 + [dma((2,))],
        (emission, reflect.reshape(-1, 128), view_grads[0, 0], meta, form, rows_perm, lanes_perm),
        remote=0,
    )
    group = n_x * size

    def forward(sources):
        return call(
            functools.partial(forward_local, slots),
            [(blocks(3 * rows), BF16)],
            [pltpu.VMEM(blocks(3 * rows), F32)],
            (index, fwd_form, sources),
            smem=1,
        )[0]

    bufs = [
        pltpu.VMEM(blocks(3 * group), BF16),
        pltpu.VMEM((2,) + blocks(group), BF16),
        pltpu.VMEM((2,) + blocks(group), BF16),
        pltpu.VMEM((n_x - 1,) + blocks(size), F32),
        pltpu.VMEM((n_x - 1,) + blocks(size), F32),
        pltpu.VMEM(blocks(rows), F32),
        pltpu.VMEM(blocks(group), F32),
        pltpu.VMEM((n_x - 1,) + blocks(size), F32),
        pltpu.VMEM((n_x - 1,) + blocks(size), F32),
    ]
    first_sums, bounced, adjoint_one, next_vector = call(
        functools.partial(middle_kernel, slots, n_x, n_s),
        [
            (blocks(size), F32),
            (blocks(rows), BF16),
            (blocks(size), F32),
            (blocks(3 * rows), BF16),
        ],
        bufs + [dma((9 + 8 * n_x,))] * 2,
        (index, forward(src), src, gain, vector, adj_form),
        smem=1,
        remote=1,
    )
    grad_emission, grad_reflect = call(
        functools.partial(end_kernel, slots, n_x, n_s),
        [((size, BLK * CONF), F32), ((size // 2, 128), F32)],
        bufs + [dma((5 + 4 * n_x,))] * 2,
        (index, forward(bounced), next_vector, adj_form, first_sums, adjoint_one, view_total),
        smem=1,
        remote=2,
    )
    return grad_emission, grad_reflect.reshape(size * BLK)


def solution(mesh):
    in_specs = (
        P(("level", "space", "col"), None),
        P(("level", "space", "col")),
        P(("level", "space"), "col", None, None),
        P(("level", "space"), "col", None),
        P(("level", "space"), "col", None, None, None),
        P(("level", "space"), "col", None, None),
        P(("level", "space"), "col", None),
    )
    out_specs = (P(("level", "space", "col"), None), P(("level", "space", "col")))
    step = functools.partial(body, mesh.shape["space"], mesh.shape["col"])
    return jax.shard_map(step, mesh=mesh, in_specs=in_specs, out_specs=out_specs, check_vma=False)
```

```python
import functools

import jax
import jax.numpy as jnp
from jax import lax
from jax.experimental import pallas as pl
from jax.experimental.pallas import tpu as pltpu
from jax.sharding import PartitionSpec as P

BLK = 64
CONF = 64
PK = BLK * CONF // 128
MESH = pl.DeviceIdType.MESH
F32 = jnp.float32
BF16 = jnp.bfloat16
VMEM_BYTES = 32 * 1024 * 1024
FIRST_BYTES = 44 * 1024 * 1024


class Net:
    def __init__(self, send_sems, recv_sems):
        self.send_sems, self.recv_sems, self.used = send_sems, recv_sems, 0

    def copy(self, src, dst, target):
        n = self.used
        self.used += 1
        return pltpu.make_async_remote_copy(
            src_ref=src,
            dst_ref=dst,
            send_sem=self.send_sems.at[n],
            recv_sem=self.recv_sems.at[n],
            device_id=target,
            device_id_type=MESH,
        )


def place():
    col = lax.axis_index("col")
    return lax.axis_index("space"), col // 2, col % 2


def greet(n_x, z_all, n_s):
    s, x, core = place()
    barrier = pltpu.get_barrier_semaphore()
    targets = [{"col": 2 * x + 1 - core}]
    targets += [{"col": 2 * ((x + d) % n_x) + core} for d in range(1, n_x)]
    if z_all:
        targets += [{"space": (s + d) % n_s} for d in range(1, n_s)]
    for target in targets:
        pl.semaphore_signal(barrier, inc=1, device_id=target, device_id_type=MESH)
    if not z_all:

        @pl.when(s > 0)
        def _():
            pl.semaphore_signal(barrier, inc=1, device_id={"space": s - 1}, device_id_type=MESH)

        @pl.when(s < n_s - 1)
        def _():
            pl.semaphore_signal(barrier, inc=1, device_id={"space": s + 1}, device_id_type=MESH)

    if z_all:
        pl.semaphore_wait(barrier, len(targets))
    else:
        sides = (s > 0).astype(jnp.int32) + (s < n_s - 1).astype(jnp.int32)
        pl.semaphore_wait(barrier, len(targets) + sides)


def low_half(rows):
    return lax.broadcasted_iota(jnp.int32, (rows, 128), 1) < 64


class GatherCol:
    def __init__(self, net, buf, n_x, size, base=0):
        s, x, core = place()
        self.net, self.buf, self.n_x, self.size, self.base = net, buf, n_x, size, base
        self.x, self.core = x, core
        mine = self.piece(core, x)
        self.across = []
        for d in range(1, n_x):
            self.across.append(net.copy(mine, mine, {"col": 2 * ((x + d) % n_x) + core}))
        self.beside = [net.copy(mine, mine, {"col": 2 * x + 1 - core})]
        for cp in self.across + self.beside:
            cp.start()

    def piece(self, core, x):
        return self.buf.at[pl.ds(self.base + (core * self.n_x + x) * self.size, self.size)]

    def arrive_across(self):
        for d, cp in enumerate(self.across, 1):
            cp.wait_recv()
            got = self.piece(self.core, (self.x + self.n_x - d) % self.n_x)
            on = self.net.copy(got, got, {"col": 2 * self.x + 1 - self.core})
            on.start()
            self.beside.append(on)

    def finish(self):
        for cp in self.beside:
            cp.wait_recv()
        for cp in self.beside + self.across:
            cp.wait_send()


class GatherWindow:
    def __init__(self, net, buf, n_x, size, n_s):
        s, x, core = place()
        self.net, self.buf, self.n_x, self.size, self.n_s = net, buf, n_x, size, n_s
        self.x, self.core = x, core
        self.z, self.beside = [], []
        self.across = []
        mine = self.piece(1, x)
        for d in range(1, n_x):
            cp = net.copy(mine, mine, {"col": 2 * ((x + d) % n_x) + core})
            cp.start()
            self.across.append(cp)
        self.along(x)
        self.pass_on(mine)

    def piece(self, run, x):
        start = ((2 * run + self.core) * self.n_x + x) * self.size
        return self.buf.at[pl.ds(start, self.size)]

    def pass_on(self, piece):
        cp = self.net.copy(piece, piece, {"col": 2 * self.x + 1 - self.core})
        cp.start()
        self.beside.append(cp)

    def along(self, x):
        s = lax.axis_index("space")
        up = self.net.copy(self.piece(1, x), self.piece(0, x), {"space": s + 1})
        down = self.net.copy(self.piece(1, x), self.piece(2, x), {"space": s - 1})
        pl.when(s < self.n_s - 1)(up.start)
        pl.when(s > 0)(down.start)
        self.z.append((up, down, x))

    def arrive_across(self):
        for d, cp in enumerate(self.across, 1):
            cp.wait_recv()
            at = (self.x + self.n_x - d) % self.n_x
            self.along(at)
            self.pass_on(self.piece(1, at))

    def finish(self):
        s = lax.axis_index("space")
        below, above = s > 0, s < self.n_s - 1
        other = {"col": 2 * self.x + 1 - self.core}
        for up, down, x in self.z:
            before = self.net.copy(self.piece(0, x), self.piece(0, x), other)
            after = self.net.copy(self.piece(2, x), self.piece(2, x), other)
            for there, came, on in ((below, up, before), (above, down, after)):

                @pl.when(there)
                def _(came=came, on=on):
                    came.wait_recv()
                    on.start()

            pl.when(above)(up.wait_send)
            pl.when(below)(down.wait_send)
            self.beside.append((below, before))
            self.beside.append((above, after))
        for cp in self.beside:
            if isinstance(cp, tuple):
                pl.when(cp[0])(cp[1].wait)
            else:
                cp.wait()
        for cp in self.across:
            cp.wait_send()


class SumForward:
    def __init__(self, net, part, got_core, z_out, z_in, x_out, x_in, n_x, size, n_s):
        s, x, core = place()
        self.net, self.part, self.got_core = net, part, got_core
        self.z_out, self.z_in, self.x_out, self.x_in = z_out, z_in, x_out, x_in
        self.n_x, self.size, self.n_s = n_x, size, n_s
        self.order = [(x + d) % n_x for d in list(range(1, n_x)) + [0]]
        self.first, self.z = {}, []
        for d, to in enumerate(self.order):
            for r in (0, 2, 1):
                src = part.at[pl.ds(((2 * r + 1 - core) * n_x + to) * size, size)]
                dst = got_core.at[pl.ds((r * n_x + to) * size, size)]
                cp = net.copy(src, dst, {"col": 2 * x + 1 - core})
                cp.start()
                self.first[d, r] = cp

    def pair(self, r, at):
        s, x, core = place()
        n_x, size = self.n_x, self.size
        mine = self.part[pl.ds(((2 * r + core) * n_x + at) * size, size)]
        return mine.astype(F32) + self.got_core[pl.ds((r * n_x + at) * size, size)].astype(F32)

    def along(self):
        s, x, core = place()
        for side, edge in ((0, s == 0), (1, s == self.n_s - 1)):

            @pl.when(edge)
            def _(side=side):
                self.z_in[side] = jnp.zeros(self.z_in.shape[1:], BF16)

        for d, to in enumerate(self.order):
            rows = pl.ds(to * self.size, self.size)
            down = self.net.copy(self.z_out.at[0, rows], self.z_in.at[1, rows], {"space": s - 1})
            up = self.net.copy(self.z_out.at[1, rows], self.z_in.at[0, rows], {"space": s + 1})
            self.first[d, 0].wait_recv()

            @pl.when(s > 0)
            def _(down=down, rows=rows, to=to):
                self.z_out[0, rows] = self.pair(0, to).astype(BF16)
                down.start()

            self.first[d, 2].wait_recv()

            @pl.when(s < self.n_s - 1)
            def _(up=up, rows=rows, to=to):
                self.z_out[1, rows] = self.pair(2, to).astype(BF16)
                up.start()

            self.z.append((down, up))

    def rows(self, d):
        s, x, core = place()
        self.first[d, 1].wait_recv()
        down, up = self.z[d]
        pl.when(s > 0)(up.wait_recv)
        pl.when(s < self.n_s - 1)(down.wait_recv)
        at = self.order[d]
        total = self.pair(1, at)
        for side in range(2):
            total = total + self.z_in[side, pl.ds(at * self.size, self.size)].astype(F32)
        return total

    def across(self):
        s, x, core = place()
        self.x = []
        for d in range(self.n_x - 1):
            self.x_out[d] = self.rows(d)
            to = {"col": 2 * self.order[d] + core}
            cp = self.net.copy(self.x_out.at[d], self.x_in.at[d], to)
            cp.start()
            self.x.append(cp)

    def finish(self):
        s, x, core = place()
        total = self.rows(self.n_x - 1)
        for d in range(self.n_x - 1):
            self.x[d].wait_recv()
            total = total + self.x_in[d]
        for cp in list(self.first.values()) + self.x:
            cp.wait_send()
        for down, up in self.z:
            pl.when(s > 0)(down.wait_send)
            pl.when(s < self.n_s - 1)(up.wait_send)
        return total


class SumCol:
    def __init__(self, net, part, got_core, x_out, x_in, n_x, size):
        s, x, core = place()
        self.net, self.part, self.got_core = net, part, got_core
        self.x_out, self.x_in, self.n_x, self.size = x_out, x_in, n_x, size
        self.group = n_x * size
        self.first = []
        for d in list(range(1, n_x)) + [0]:
            to = (x + d) % n_x
            src = part.at[pl.ds((1 - core) * self.group + to * size, size)]
            cp = net.copy(src, got_core.at[pl.ds(to * size, size)], {"col": 2 * x + 1 - core})
            cp.start()
            self.first.append(cp)

    def rows(self, at):
        s, x, core = place()
        mine = self.part[pl.ds(core * self.group + at * self.size, self.size)]
        return mine + self.got_core[pl.ds(at * self.size, self.size)]

    def across(self):
        s, x, core = place()
        self.x = []
        for d in range(1, self.n_x):
            to = (x + d) % self.n_x
            self.first[d - 1].wait_recv()
            self.x_out[d - 1] = self.rows(to)
            cp = self.net.copy(self.x_out.at[d - 1], self.x_in.at[d - 1], {"col": 2 * to + core})
            cp.start()
            self.x.append(cp)

    def finish(self):
        s, x, core = place()
        self.first[-1].wait_recv()
        total = self.rows(x)
        for d in range(1, self.n_x):
            self.x[d - 1].wait_recv()
            total = total + self.x_in[d - 1]
        for cp in self.first + self.x:
            cp.wait_send()
        return total


def patch_masks(p):
    i = lax.broadcasted_iota(jnp.int32, (PK, 128), 0)
    t = lax.broadcasted_iota(jnp.int32, (PK, 128), 1)
    rows = t == (p % 2) * 64 + 2 * i + t % 2
    patch = lax.broadcasted_iota(jnp.int32, (128, 128), 0)
    lane = lax.broadcasted_iota(jnp.int32, (128, 128), 1)
    return rows, (patch % 2 == lane // 64).astype(F32)


def start_kernel(
    n_x, n_s, emission_in, view, form_in, reflect, meta, rows_perm, lanes_perm,
    src, fwd_form, adj_form, gain, view_total, vector,
    emission, form, views, metas, entries, unpacked, send_sems, recv_sems, local_sem,
):
    s, x, core = place()
    size = emission.shape[0]
    cap = view.shape[1]
    rows = form.shape[0]
    net = Net(send_sems, recv_sems)
    where = core * n_x + x
    bring = pltpu.make_async_copy(emission_in, emission, local_sem.at[2])
    bring.start()
    bring_form = pltpu.make_async_copy(form_in, form, local_sem.at[3])
    bring_form.start()
    greet(n_x, True, n_s)
    at = where * n_s + s
    spread = []
    for d in range(1, n_s):
        to = (s + d) % n_s
        spread.append(net.copy(view.at[to], views.at[at], {"space": to}))
        spread.append(net.copy(meta.at[to], metas.at[at], {"space": to}))
    for cp in spread:
        cp.start()
    bring.wait()
    for i in range(PK):
        unpacked[:, i, :] = emission[:, i * 128 : (i + 1) * 128].astype(F32)
    src[pl.ds(where * size, size)] = unpacked[...].astype(BF16)
    own_view = pltpu.make_async_copy(view.at[s], views.at[at], local_sem.at[0])
    own_view.start()
    own_meta = pltpu.make_async_copy(meta.at[s], metas.at[at], local_sem.at[1])
    own_meta.start()
    gather = GatherCol(net, src, n_x, size)

    def prepare(j):
        c, r = j // size, j % size
        to = ((c % 2) * n_x + c // 2) * size + r
        plain = jnp.dot(rows_perm[...], form[j], preferred_element_type=F32).astype(BF16)
        fwd_form[to] = jnp.dot(plain, lanes_perm[...], preferred_element_type=F32).astype(BF16)
        adj_form[to] = lax.dot_general(
            lanes_perm[...], plain, (((0,), (1,)), ((), ())), preferred_element_type=F32
        ).astype(BF16)

    bring_form.wait()
    loop(0, rows // 4, prepare, 8)
    for p in range(size):
        sel, lanes = patch_masks(p)
        picked = jnp.where(sel, reflect[p // 2 : p // 2 + 1, :], 0.0)
        gain[p] = jnp.dot(
            picked, lanes, preferred_element_type=F32, precision=lax.Precision.HIGHEST
        )
    own_view.wait()
    own_meta.wait()
    for cp in spread:
        cp.wait_recv()
    more = [GatherCol(net, views, n_x, n_s), GatherCol(net, metas, n_x, n_s)]
    gather.arrive_across()
    loop(rows // 4, rows // 4, prepare, 8)
    for g in more:
        g.arrive_across()
    gather.finish()
    for g in more:
        g.finish()
    count = views.shape[0] * cap
    for t in range(views.shape[0]):
        entries[t * cap : (t + 1) * cap, :] = views[t].astype(F32)
    marks = jnp.sum(metas[...], axis=0)
    wanted = lax.broadcasted_iota(jnp.int32, (size, marks.shape[1]), 0) + (2 * x + core) * size + 1
    chosen = (wanted == marks).astype(F32).astype(BF16)[:, :count]
    for i in range(0, PK, 4):
        cut = entries[:, i * 128 : (i + 4) * 128].astype(BF16)
        found = jnp.dot(chosen, cut, preferred_element_type=F32)
        for u in range(4):
            view_total[:, i + u, :] = found[:, u * 128 : (u + 1) * 128]
    vector[pl.ds(2 * n_x * size + where * size, size)] = (gain[...] * view_total[...]).astype(BF16)
    window = GatherWindow(net, vector, n_x, size, n_s)
    loop(rows // 2, rows // 4, prepare, 8)
    window.arrive_across()
    loop(rows // 2 + rows // 4, rows // 4, prepare, 8)
    window.finish()
    for cp in spread:
        cp.wait_send()


def forward_step(j, form, src, index, slots, window):
    low = low_half(PK)
    piece = src[j].astype(F32)
    turned = pltpu.roll(piece, 64, 1)
    zero = jnp.zeros_like(piece)
    wide = jnp.concatenate(
        [
            jnp.where(low, piece, zero),
            jnp.where(low, turned, zero),
            jnp.where(low, zero, turned),
            jnp.where(low, zero, piece),
        ],
        axis=0,
    ).astype(BF16)
    terms = jnp.dot(form[j], wide, preferred_element_type=F32)
    for k in range(slots):
        at = index[j * slots + k]
        window[at] = window[at] + terms[k * PK : (k + 1) * PK]


def adjoint_step(j, form, vector, index, slots, out):
    low = low_half(PK)
    picked = jnp.concatenate([vector[index[j * slots + k]] for k in range(slots)], axis=0)
    m = jnp.dot(form[j], picked, preferred_element_type=F32)
    even = m[:PK] + pltpu.roll(m[2 * PK : 3 * PK], 64, 1)
    odd = pltpu.roll(m[PK : 2 * PK], 64, 1) + m[3 * PK :]
    out[j] = jnp.where(low, even, odd)


def loop(first, count, step, unroll):
    def body(t, carry):
        for u in range(unroll):
            step(first + t * unroll + u)
        return carry

    lax.fori_loop(0, count // unroll, body, 0)


def clear(window):
    def body(t, carry):
        window[pl.ds(t * 8, 8)] = jnp.zeros((8,) + window.shape[1:], F32)
        return carry

    lax.fori_loop(0, window.shape[0] // 8, body, 0)


def write_part(window, part):
    def body(t, carry):
        part[pl.ds(t * 8, 8)] = window[pl.ds(t * 8, 8)].astype(BF16)
        return carry

    lax.fori_loop(0, window.shape[0] // 8, body, 0)


def forward_local(slots, index, form, src, part, window):
    clear(window)
    loop(0, form.shape[0], lambda j: forward_step(j, form, src, index, slots, window), 8)
    write_part(window, part)


def middle_kernel(
    slots, n_x, n_s, index, part, src, gain, vector, adj_form,
    first_sums, bounced, adjoint_one, next_vector,
    got_core, z_out, z_in, x_out, x_in,
    terms, one_core, one_out, one_in, send_sems, recv_sems,
):
    s, x, core = place()
    size = gain.shape[0]
    net = Net(send_sems, recv_sems)
    greet(n_x, False, n_s)
    mine = (core * n_x + x) * size
    group = n_x * size
    step = lambda j: adjoint_step(j, adj_form, vector, index, slots, terms)
    sums = SumForward(net, part, got_core, z_out, z_in, x_out, x_in, n_x, size, n_s)
    loop((1 - core) * group, group, step, 8)
    one = SumCol(net, terms, one_core, one_out, one_in, n_x, size)
    sums.along()
    loop(core * group, group, step, 8)
    one.across()
    sums.across()
    adjoint_one[...] = one.finish()
    next_vector[pl.ds(2 * group + mine, size)] = (gain[...] * adjoint_one[...]).astype(BF16)
    gather = GatherWindow(net, next_vector, n_x, size, n_s)
    first_sums[...] = sums.finish()
    bounced[pl.ds(mine, size)] = (
        src[pl.ds(mine, size)].astype(F32) + gain[...] * first_sums[...]
    ).astype(BF16)
    second = GatherCol(net, bounced, n_x, size)
    gather.arrive_across()
    second.arrive_across()
    gather.finish()
    second.finish()


def end_kernel(
    slots, n_x, n_s, index, part, vector, adj_form, first_sums, adjoint_one, view_total,
    grad_emission, grad_reflect,
    got_core, z_out, z_in, x_out, x_in,
    terms, two_core, two_out, two_in, send_sems, recv_sems,
):
    s, x, core = place()
    size = view_total.shape[0]
    net = Net(send_sems, recv_sems)
    greet(n_x, False, n_s)
    group = n_x * size
    step = lambda j: adjoint_step(j, adj_form, vector, index, slots, terms)
    sums = SumForward(net, part, got_core, z_out, z_in, x_out, x_in, n_x, size, n_s)
    loop((1 - core) * group, group, step, 8)
    two = SumCol(net, terms, two_core, two_out, two_in, n_x, size)
    sums.along()
    loop(core * group, group, step, 8)
    two.across()
    sums.across()
    got_two = two.finish()
    keep = two_core
    keep[pl.ds(0, size)] = view_total[...] + adjoint_one[...] + got_two
    for i in range(PK):
        grad_emission[:, i * 128 : (i + 1) * 128] = keep[:size, i, :]
    keep[pl.ds(0, size)] = view_total[...] * sums.finish() + adjoint_one[...] * first_sums[...]
    for p in range(0, size, 2):
        total = jnp.zeros((1, 128), F32)
        for q in (p, p + 1):
            sel, lanes = patch_masks(q)
            spread = lax.dot_general(
                keep[q], lanes, (((1,), (1,)), ((), ())),
                preferred_element_type=F32, precision=lax.Precision.HIGHEST,
            )
            total = total + jnp.sum(jnp.where(sel, spread, 0.0), axis=0, keepdims=True)
        grad_reflect[p // 2 : p // 2 + 1, :] = total


def call(kernel, outs, scratch, operands, smem=0, hbm=0, remote=None, vmem_bytes=VMEM_BYTES):
    vmem = pl.BlockSpec(memory_space=pltpu.VMEM)
    specs = [pl.BlockSpec(memory_space=pltpu.SMEM)] * smem
    specs += [pl.BlockSpec(memory_space=pltpu.HBM)] * hbm
    specs += [vmem] * (len(operands) - smem - hbm)
    if remote is None:
        params = pltpu.CompilerParams(vmem_limit_bytes=vmem_bytes)
    else:
        params = pltpu.CompilerParams(
            vmem_limit_bytes=vmem_bytes, collective_id=remote, has_side_effects=True
        )
    return pl.pallas_call(
        kernel,
        out_shape=[jax.ShapeDtypeStruct(*out) for out in outs],
        in_specs=specs,
        out_specs=[vmem] * len(outs),
        scratch_shapes=scratch,
        compiler_params=params,
    )(*operands)


def body(n_s, n_c, emission, reflect, form_blocks, block_rows, view_grads, view_rows, view_counts):
    n_x = n_c // 2
    rows, slots = form_blocks.shape[0], form_blocks.shape[2]
    size = emission.shape[0]
    cap = view_grads.shape[3]
    s = lax.axis_index("space")
    tall = slots * PK
    form = form_blocks.reshape(rows, slots, PK, 128).transpose(0, 2, 1, 3).reshape(rows, tall, 128)
    a, b = jnp.arange(tall)[:, None], jnp.arange(tall)[None, :]
    rows_perm = ((a % PK) * slots + a // PK == b).astype(BF16)
    q, p = jnp.arange(128)[:, None], jnp.arange(128)[None, :]
    lanes_perm = (q == (p // 64) * 64 + 2 * (p % 32) + (p % 64) // 32).astype(BF16)
    target = block_rows.reshape(rows, slots) - (s - 1) * rows
    block = target % rows
    piece = block // size
    target = target - block + ((piece % 2) * n_x + piece // 2) * size + block % size
    index = target.reshape(n_x, 2, size, slots).transpose(1, 0, 2, 3).reshape(rows * slots)
    col = lax.axis_index("col")
    lists = n_c * n_s
    at = ((col % 2) * n_x + col // 2) * n_s + s
    live = jnp.arange(cap, dtype=jnp.int32) < view_counts[0, 0][:, None]
    marks = jnp.where(live, view_rows[0, 0] + 1, 0)[:, None, :]
    own_list = jnp.arange(lists, dtype=jnp.int32)[None, :, None] == at
    meta = jnp.where(own_list, marks, 0).reshape(n_s, lists * cap)
    meta = jnp.pad(meta, ((0, 0), (0, -(lists * cap) % 128)))[:, None, :]

    dma = pltpu.SemaphoreType.DMA
    blocks = lambda n: (n, PK, 128)
    src, fwd_form, adj_form, gain, view_total, vector = call(
        functools.partial(start_kernel, n_x, n_s),
        [
            (blocks(rows), BF16),
            ((rows, tall, 128), BF16),
            ((rows, 128, tall), BF16),
            (blocks(size), F32),
            (blocks(size), F32),
            (blocks(3 * rows), BF16),
        ],
        [
            pltpu.VMEM(emission.shape, BF16),
            pltpu.VMEM(form.shape, BF16),
            pltpu.VMEM((lists, cap, BLK * CONF), BF16),
            pltpu.VMEM((lists,) + meta.shape[1:], jnp.int32),
            pltpu.VMEM((lists * cap, BLK * CONF), F32),
            pltpu.VMEM(blocks(size), F32),
        ]
        + [dma((2 * n_s + 12 * n_x,))] * 2 + [dma((4,))],
        (emission, view_grads[0, 0], form, reflect.reshape(-1, 128), meta, rows_perm, lanes_perm),
        hbm=3,
        vmem_bytes=FIRST_BYTES,
        remote=0,
    )
    group = n_x * size

    def forward(sources):
        return call(
            functools.partial(forward_local, slots),
            [(blocks(3 * rows), BF16)],
            [pltpu.VMEM(blocks(3 * rows), F32)],
            (index, fwd_form, sources),
            smem=1,
        )[0]

    bufs = [
        pltpu.VMEM(blocks(3 * group), BF16),
        pltpu.VMEM((2,) + blocks(group), BF16),
        pltpu.VMEM((2,) + blocks(group), BF16),
        pltpu.VMEM((n_x - 1,) + blocks(size), F32),
        pltpu.VMEM((n_x - 1,) + blocks(size), F32),
        pltpu.VMEM(blocks(rows), F32),
        pltpu.VMEM(blocks(group), F32),
        pltpu.VMEM((n_x - 1,) + blocks(size), F32),
        pltpu.VMEM((n_x - 1,) + blocks(size), F32),
    ]
    first_sums, bounced, adjoint_one, next_vector = call(
        functools.partial(middle_kernel, slots, n_x, n_s),
        [
            (blocks(size), F32),
            (blocks(rows), BF16),
            (blocks(size), F32),
            (blocks(3 * rows), BF16),
        ],
        bufs + [dma((16 * n_x,))] * 2,
        (index, forward(src), src, gain, vector, adj_form),
        smem=1,
        remote=1,
    )
    grad_emission, grad_reflect = call(
        functools.partial(end_kernel, slots, n_x, n_s),
        [((size, BLK * CONF), F32), ((size // 2, 128), F32)],
        bufs + [dma((8 * n_x,))] * 2,
        (index, forward(bounced), next_vector, adj_form, first_sums, adjoint_one, view_total),
        smem=1,
        remote=2,
    )
    return grad_emission, grad_reflect.reshape(size * BLK)


def solution(mesh):
    in_specs = (
        P(("level", "space", "col"), None),
        P(("level", "space", "col")),
        P(("level", "space"), "col", None, None),
        P(("level", "space"), "col", None),
        P(("level", "space"), "col", None, None, None),
        P(("level", "space"), "col", None, None),
        P(("level", "space"), "col", None),
    )
    out_specs = (P(("level", "space", "col"), None), P(("level", "space", "col")))
    step = functools.partial(body, mesh.shape["space"], mesh.shape["col"])
    return jax.shard_map(step, mesh=mesh, in_specs=in_specs, out_specs=out_specs, check_vma=False)
```

```python
import functools

import jax
import jax.numpy as jnp
from jax import lax
from jax.experimental import pallas as pl
from jax.experimental.pallas import tpu as pltpu
from jax.sharding import PartitionSpec as P

BLK = 64
CONF = 64
PK = BLK * CONF // 128
MESH = pl.DeviceIdType.MESH
F32 = jnp.float32
BF16 = jnp.bfloat16
VMEM_BYTES = 32 * 1024 * 1024
FIRST_BYTES = 48 * 1024 * 1024


class Net:
    def __init__(self, send_sems, recv_sems):
        self.send_sems, self.recv_sems, self.used = send_sems, recv_sems, 0

    def copy(self, src, dst, target):
        n = self.used
        self.used += 1
        return pltpu.make_async_remote_copy(
            src_ref=src,
            dst_ref=dst,
            send_sem=self.send_sems.at[n],
            recv_sem=self.recv_sems.at[n],
            device_id=target,
            device_id_type=MESH,
        )


def place():
    col = lax.axis_index("col")
    return lax.axis_index("space"), col // 2, col % 2


def greet(n_x, z_all, n_s):
    s, x, core = place()
    barrier = pltpu.get_barrier_semaphore()
    targets = [{"col": 2 * x + 1 - core}]
    targets += [{"col": 2 * ((x + d) % n_x) + core} for d in range(1, n_x)]
    if z_all:
        targets += [{"space": (s + d) % n_s} for d in range(1, n_s)]
    for target in targets:
        pl.semaphore_signal(barrier, inc=1, device_id=target, device_id_type=MESH)
    if not z_all:

        @pl.when(s > 0)
        def _():
            pl.semaphore_signal(barrier, inc=1, device_id={"space": s - 1}, device_id_type=MESH)

        @pl.when(s < n_s - 1)
        def _():
            pl.semaphore_signal(barrier, inc=1, device_id={"space": s + 1}, device_id_type=MESH)

    if z_all:
        pl.semaphore_wait(barrier, len(targets))
    else:
        sides = (s > 0).astype(jnp.int32) + (s < n_s - 1).astype(jnp.int32)
        pl.semaphore_wait(barrier, len(targets) + sides)


def low_half(rows):
    return lax.broadcasted_iota(jnp.int32, (rows, 128), 1) < 64


class GatherCol:
    def __init__(self, net, buf, n_x, size, base=0):
        s, x, core = place()
        self.net, self.buf, self.n_x, self.size, self.base = net, buf, n_x, size, base
        self.x, self.core = x, core
        mine = self.piece(core, x)
        self.across = []
        for d in range(1, n_x):
            self.across.append(net.copy(mine, mine, {"col": 2 * ((x + d) % n_x) + core}))
        self.beside = [net.copy(mine, mine, {"col": 2 * x + 1 - core})]
        for cp in self.across + self.beside:
            cp.start()

    def piece(self, core, x):
        return self.buf.at[pl.ds(self.base + (core * self.n_x + x) * self.size, self.size)]

    def arrive_across(self):
        for d, cp in enumerate(self.across, 1):
            cp.wait_recv()
            got = self.piece(self.core, (self.x + self.n_x - d) % self.n_x)
            on = self.net.copy(got, got, {"col": 2 * self.x + 1 - self.core})
            on.start()
            self.beside.append(on)

    def finish(self):
        for cp in self.beside:
            cp.wait_recv()
        for cp in self.beside + self.across:
            cp.wait_send()


class GatherWindow:
    def __init__(self, net, buf, n_x, size, n_s):
        s, x, core = place()
        self.net, self.buf, self.n_x, self.size, self.n_s = net, buf, n_x, size, n_s
        self.x, self.core = x, core
        self.z, self.beside = [], []
        self.across = []
        mine = self.piece(1, x)
        for d in range(1, n_x):
            cp = net.copy(mine, mine, {"col": 2 * ((x + d) % n_x) + core})
            cp.start()
            self.across.append(cp)
        self.along(x)
        self.pass_on(mine)

    def piece(self, run, x):
        start = ((2 * run + self.core) * self.n_x + x) * self.size
        return self.buf.at[pl.ds(start, self.size)]

    def pass_on(self, piece):
        cp = self.net.copy(piece, piece, {"col": 2 * self.x + 1 - self.core})
        cp.start()
        self.beside.append(cp)

    def along(self, x):
        s = lax.axis_index("space")
        up = self.net.copy(self.piece(1, x), self.piece(0, x), {"space": s + 1})
        down = self.net.copy(self.piece(1, x), self.piece(2, x), {"space": s - 1})
        pl.when(s < self.n_s - 1)(up.start)
        pl.when(s > 0)(down.start)
        self.z.append((up, down, x))

    def arrive_across(self):
        for d, cp in enumerate(self.across, 1):
            cp.wait_recv()
            at = (self.x + self.n_x - d) % self.n_x
            self.along(at)
            self.pass_on(self.piece(1, at))

    def finish(self):
        s = lax.axis_index("space")
        below, above = s > 0, s < self.n_s - 1
        other = {"col": 2 * self.x + 1 - self.core}
        for up, down, x in self.z:
            before = self.net.copy(self.piece(0, x), self.piece(0, x), other)
            after = self.net.copy(self.piece(2, x), self.piece(2, x), other)
            for there, came, on in ((below, up, before), (above, down, after)):

                @pl.when(there)
                def _(came=came, on=on):
                    came.wait_recv()
                    on.start()

            pl.when(above)(up.wait_send)
            pl.when(below)(down.wait_send)
            self.beside.append((below, before))
            self.beside.append((above, after))
        for cp in self.beside:
            if isinstance(cp, tuple):
                pl.when(cp[0])(cp[1].wait)
            else:
                cp.wait()
        for cp in self.across:
            cp.wait_send()


class SumForward:
    def __init__(self, net, part, got_core, z_out, z_in, x_out, x_in, n_x, size, n_s):
        s, x, core = place()
        self.net, self.part, self.got_core = net, part, got_core
        self.z_out, self.z_in, self.x_out, self.x_in = z_out, z_in, x_out, x_in
        self.n_x, self.size, self.n_s = n_x, size, n_s
        self.order = [(x + d) % n_x for d in list(range(1, n_x)) + [0]]
        self.first, self.z = {}, []
        for d, to in enumerate(self.order):
            for r in (0, 2, 1):
                src = part.at[pl.ds(((2 * r + 1 - core) * n_x + to) * size, size)]
                dst = got_core.at[pl.ds((r * n_x + to) * size, size)]
                cp = net.copy(src, dst, {"col": 2 * x + 1 - core})
                cp.start()
                self.first[d, r] = cp

    def pair(self, r, at):
        s, x, core = place()
        n_x, size = self.n_x, self.size
        mine = self.part[pl.ds(((2 * r + core) * n_x + at) * size, size)]
        return mine.astype(F32) + self.got_core[pl.ds((r * n_x + at) * size, size)].astype(F32)

    def along(self):
        s, x, core = place()
        for side, edge in ((0, s == 0), (1, s == self.n_s - 1)):

            @pl.when(edge)
            def _(side=side):
                self.z_in[side] = jnp.zeros(self.z_in.shape[1:], BF16)

        for d, to in enumerate(self.order):
            rows = pl.ds(to * self.size, self.size)
            down = self.net.copy(self.z_out.at[0, rows], self.z_in.at[1, rows], {"space": s - 1})
            up = self.net.copy(self.z_out.at[1, rows], self.z_in.at[0, rows], {"space": s + 1})
            self.first[d, 0].wait_recv()

            @pl.when(s > 0)
            def _(down=down, rows=rows, to=to):
                self.z_out[0, rows] = self.pair(0, to).astype(BF16)
                down.start()

            self.first[d, 2].wait_recv()

            @pl.when(s < self.n_s - 1)
            def _(up=up, rows=rows, to=to):
                self.z_out[1, rows] = self.pair(2, to).astype(BF16)
                up.start()

            self.z.append((down, up))

    def rows(self, d):
        s, x, core = place()
        self.first[d, 1].wait_recv()
        down, up = self.z[d]
        pl.when(s > 0)(up.wait_recv)
        pl.when(s < self.n_s - 1)(down.wait_recv)
        at = self.order[d]
        total = self.pair(1, at)
        for side in range(2):
            total = total + self.z_in[side, pl.ds(at * self.size, self.size)].astype(F32)
        return total

    def across(self):
        s, x, core = place()
        self.x = []
        for d in range(self.n_x - 1):
            self.x_out[d] = self.rows(d)
            to = {"col": 2 * self.order[d] + core}
            cp = self.net.copy(self.x_out.at[d], self.x_in.at[d], to)
            cp.start()
            self.x.append(cp)

    def finish(self):
        s, x, core = place()
        total = self.rows(self.n_x - 1)
        for d in range(self.n_x - 1):
            self.x[d].wait_recv()
            total = total + self.x_in[d]
        for cp in list(self.first.values()) + self.x:
            cp.wait_send()
        for down, up in self.z:
            pl.when(s > 0)(down.wait_send)
            pl.when(s < self.n_s - 1)(up.wait_send)
        return total


class SumCol:
    def __init__(self, net, part, got_core, x_out, x_in, n_x, size):
        s, x, core = place()
        self.net, self.part, self.got_core = net, part, got_core
        self.x_out, self.x_in, self.n_x, self.size = x_out, x_in, n_x, size
        self.group = n_x * size
        self.first = []
        for d in list(range(1, n_x)) + [0]:
            to = (x + d) % n_x
            src = part.at[pl.ds((1 - core) * self.group + to * size, size)]
            cp = net.copy(src, got_core.at[pl.ds(to * size, size)], {"col": 2 * x + 1 - core})
            cp.start()
            self.first.append(cp)

    def rows(self, at):
        s, x, core = place()
        mine = self.part[pl.ds(core * self.group + at * self.size, self.size)]
        return mine + self.got_core[pl.ds(at * self.size, self.size)]

    def across(self):
        s, x, core = place()
        self.x = []
        for d in range(1, self.n_x):
            to = (x + d) % self.n_x
            self.first[d - 1].wait_recv()
            self.x_out[d - 1] = self.rows(to)
            cp = self.net.copy(self.x_out.at[d - 1], self.x_in.at[d - 1], {"col": 2 * to + core})
            cp.start()
            self.x.append(cp)

    def finish(self):
        s, x, core = place()
        self.first[-1].wait_recv()
        total = self.rows(x)
        for d in range(1, self.n_x):
            self.x[d - 1].wait_recv()
            total = total + self.x_in[d - 1]
        for cp in self.first + self.x:
            cp.wait_send()
        return total


def patch_masks(p):
    i = lax.broadcasted_iota(jnp.int32, (PK, 128), 0)
    t = lax.broadcasted_iota(jnp.int32, (PK, 128), 1)
    rows = t == (p % 2) * 64 + 2 * i + t % 2
    patch = lax.broadcasted_iota(jnp.int32, (128, 128), 0)
    lane = lax.broadcasted_iota(jnp.int32, (128, 128), 1)
    return rows, (patch % 2 == lane // 64).astype(F32)


def start_kernel(
    n_x, n_s, emission_in, view, form_in, reflect, meta, rows_perm, lanes_perm,
    src, fwd_form, adj_form, gain, view_total, vector,
    emission, form, views, metas, entries, unpacked, send_sems, recv_sems, local_sem,
):
    s, x, core = place()
    size = emission.shape[0]
    cap = view.shape[1]
    rows = form.shape[0]
    net = Net(send_sems, recv_sems)
    where = core * n_x + x
    bring = pltpu.make_async_copy(emission_in, emission, local_sem.at[2])
    bring.start()
    bring_form = pltpu.make_async_copy(form_in, form, local_sem.at[3])
    bring_form.start()
    greet(n_x, True, n_s)
    at = where * n_s + s
    spread = []
    for d in range(1, n_s):
        to = (s + d) % n_s
        spread.append(net.copy(view.at[to], views.at[at], {"space": to}))
        spread.append(net.copy(meta.at[to], metas.at[at], {"space": to}))
    for cp in spread:
        cp.start()
    bring.wait()
    for i in range(PK):
        unpacked[:, i, :] = emission[:, i * 128 : (i + 1) * 128].astype(F32)
    src[pl.ds(where * size, size)] = unpacked[...].astype(BF16)
    own_view = pltpu.make_async_copy(view.at[s], views.at[at], local_sem.at[0])
    own_view.start()
    own_meta = pltpu.make_async_copy(meta.at[s], metas.at[at], local_sem.at[1])
    own_meta.start()
    gather = GatherCol(net, src, n_x, size)

    def prepare(t):
        j = t * 8
        c, r = j // size, j % size
        to = ((c % 2) * n_x + c // 2) * size + r
        plain = [
            jnp.dot(rows_perm[...], form[j + u], preferred_element_type=F32).astype(BF16)
            for u in range(8)
        ]
        tall = jnp.concatenate(plain, axis=0)
        turned = jnp.dot(tall, lanes_perm[...], preferred_element_type=F32).astype(BF16)
        for u in range(8):
            fwd_form[to + u] = turned[u * tall.shape[0] // 8 : (u + 1) * tall.shape[0] // 8]
            adj_form[to + u] = lax.dot_general(
                lanes_perm[...], plain[u], (((0,), (1,)), ((), ())), preferred_element_type=F32
            ).astype(BF16)

    eighth = rows // 8
    bring_form.wait()
    loop(0, eighth // 4, prepare, 1)
    own_view.wait()
    own_meta.wait()
    for cp in spread:
        cp.wait_recv()
    more = [GatherCol(net, views, n_x, n_s), GatherCol(net, metas, n_x, n_s)]
    gather.arrive_across()
    picked = []
    for p in range(size):
        sel, lanes = patch_masks(p)
        picked.append(jnp.where(sel, reflect[p // 2 : p // 2 + 1, :], 0.0))
    gain[...] = jnp.dot(
        jnp.concatenate(picked, axis=0), lanes,
        preferred_element_type=F32, precision=lax.Precision.HIGHEST,
    ).reshape(gain.shape)
    loop(eighth // 4, eighth // 4, prepare, 1)
    for g in more:
        g.arrive_across()
    gather.finish()
    for g in more:
        g.finish()
    count = views.shape[0] * cap
    for t in range(views.shape[0]):
        entries[t * cap : (t + 1) * cap, :] = views[t].astype(F32)
    marks = jnp.sum(metas[...], axis=0)
    wanted = lax.broadcasted_iota(jnp.int32, (size, marks.shape[1]), 0) + (2 * x + core) * size + 1
    chosen = (wanted == marks).astype(F32).astype(BF16)[:, :count]
    for i in range(0, PK, 4):
        cut = entries[:, i * 128 : (i + 4) * 128].astype(BF16)
        found = jnp.dot(chosen, cut, preferred_element_type=F32)
        for u in range(4):
            view_total[:, i + u, :] = found[:, u * 128 : (u + 1) * 128]
    vector[pl.ds(2 * n_x * size + where * size, size)] = (gain[...] * view_total[...]).astype(BF16)
    window = GatherWindow(net, vector, n_x, size, n_s)
    loop(eighth // 2, eighth // 4, prepare, 1)
    window.arrive_across()
    loop(eighth // 2 + eighth // 4, eighth // 4, prepare, 1)
    window.finish()
    for cp in spread:
        cp.wait_send()


def forward_step(j, form, src, index, slots, window):
    low = low_half(PK)
    piece = src[j].astype(F32)
    turned = pltpu.roll(piece, 64, 1)
    zero = jnp.zeros_like(piece)
    wide = jnp.concatenate(
        [
            jnp.where(low, piece, zero),
            jnp.where(low, turned, zero),
            jnp.where(low, zero, turned),
            jnp.where(low, zero, piece),
        ],
        axis=0,
    ).astype(BF16)
    terms = jnp.dot(form[j], wide, preferred_element_type=F32)
    for k in range(slots):
        at = index[j * slots + k]
        window[at] = window[at] + terms[k * PK : (k + 1) * PK]


def adjoint_step(j, form, vector, index, slots, out):
    low = low_half(PK)
    picked = jnp.concatenate([vector[index[j * slots + k]] for k in range(slots)], axis=0)
    m = jnp.dot(form[j], picked, preferred_element_type=F32)
    even = m[:PK] + pltpu.roll(m[2 * PK : 3 * PK], 64, 1)
    odd = pltpu.roll(m[PK : 2 * PK], 64, 1) + m[3 * PK :]
    out[j] = jnp.where(low, even, odd)


def loop(first, count, step, unroll):
    def body(t, carry):
        for u in range(unroll):
            step(first + t * unroll + u)
        return carry

    lax.fori_loop(0, count // unroll, body, 0)


def clear(window):
    def body(t, carry):
        window[pl.ds(t * 8, 8)] = jnp.zeros((8,) + window.shape[1:], F32)
        return carry

    lax.fori_loop(0, window.shape[0] // 8, body, 0)


def write_part(window, part):
    def body(t, carry):
        part[pl.ds(t * 8, 8)] = window[pl.ds(t * 8, 8)].astype(BF16)
        return carry

    lax.fori_loop(0, window.shape[0] // 8, body, 0)


def forward_local(slots, index, form, src, part, window):
    clear(window)
    loop(0, form.shape[0], lambda j: forward_step(j, form, src, index, slots, window), 8)
    write_part(window, part)


def middle_kernel(
    slots, n_x, n_s, index, part, src, gain, vector, adj_form,
    first_sums, bounced, adjoint_one, next_vector,
    got_core, z_out, z_in, x_out, x_in,
    terms, one_core, one_out, one_in, send_sems, recv_sems,
):
    s, x, core = place()
    size = gain.shape[0]
    net = Net(send_sems, recv_sems)
    greet(n_x, False, n_s)
    mine = (core * n_x + x) * size
    group = n_x * size
    step = lambda j: adjoint_step(j, adj_form, vector, index, slots, terms)
    sums = SumForward(net, part, got_core, z_out, z_in, x_out, x_in, n_x, size, n_s)
    loop((1 - core) * group, group, step, 8)
    one = SumCol(net, terms, one_core, one_out, one_in, n_x, size)
    sums.along()
    loop(core * group, group, step, 8)
    one.across()
    sums.across()
    adjoint_one[...] = one.finish()
    next_vector[pl.ds(2 * group + mine, size)] = (gain[...] * adjoint_one[...]).astype(BF16)
    gather = GatherWindow(net, next_vector, n_x, size, n_s)
    first_sums[...] = sums.finish()
    bounced[pl.ds(mine, size)] = (
        src[pl.ds(mine, size)].astype(F32) + gain[...] * first_sums[...]
    ).astype(BF16)
    second = GatherCol(net, bounced, n_x, size)
    gather.arrive_across()
    second.arrive_across()
    gather.finish()
    second.finish()


def end_kernel(
    slots, n_x, n_s, index, part, vector, adj_form, first_sums, adjoint_one, view_total,
    grad_emission, grad_reflect,
    got_core, z_out, z_in, x_out, x_in,
    terms, two_core, two_out, two_in, send_sems, recv_sems,
):
    s, x, core = place()
    size = view_total.shape[0]
    net = Net(send_sems, recv_sems)
    greet(n_x, False, n_s)
    group = n_x * size
    step = lambda j: adjoint_step(j, adj_form, vector, index, slots, terms)
    sums = SumForward(net, part, got_core, z_out, z_in, x_out, x_in, n_x, size, n_s)
    loop((1 - core) * group, group, step, 8)
    two = SumCol(net, terms, two_core, two_out, two_in, n_x, size)
    sums.along()
    loop(core * group, group, step, 8)
    two.across()
    sums.across()
    got_two = two.finish()
    keep = two_core
    keep[pl.ds(0, size)] = view_total[...] + adjoint_one[...] + got_two
    for i in range(PK):
        grad_emission[:, i * 128 : (i + 1) * 128] = keep[:size, i, :]
    product = view_total[...] * sums.finish() + adjoint_one[...] * first_sums[...]
    lanes = patch_masks(0)[1]
    halves = lax.dot_general(
        product.reshape(size * PK, 128), lanes, (((1,), (1,)), ((), ())),
        preferred_element_type=F32, precision=lax.Precision.HIGHEST,
    )
    for p in range(0, size, 2):
        total = jnp.zeros((1, 128), F32)
        for q in (p, p + 1):
            sel = patch_masks(q)[0]
            part_q = jnp.where(sel, halves[q * PK : (q + 1) * PK], 0.0)
            total = total + jnp.sum(part_q, axis=0, keepdims=True)
        grad_reflect[p // 2 : p // 2 + 1, :] = total


def call(kernel, outs, scratch, operands, smem=0, hbm=0, remote=None, vmem_bytes=VMEM_BYTES):
    vmem = pl.BlockSpec(memory_space=pltpu.VMEM)
    specs = [pl.BlockSpec(memory_space=pltpu.SMEM)] * smem
    specs += [pl.BlockSpec(memory_space=pltpu.HBM)] * hbm
    specs += [vmem] * (len(operands) - smem - hbm)
    if remote is None:
        params = pltpu.CompilerParams(vmem_limit_bytes=vmem_bytes)
    else:
        params = pltpu.CompilerParams(
            vmem_limit_bytes=vmem_bytes, collective_id=remote, has_side_effects=True
        )
    return pl.pallas_call(
        kernel,
        out_shape=[jax.ShapeDtypeStruct(*out) for out in outs],
        in_specs=specs,
        out_specs=[vmem] * len(outs),
        scratch_shapes=scratch,
        compiler_params=params,
    )(*operands)


def body(n_s, n_c, emission, reflect, form_blocks, block_rows, view_grads, view_rows, view_counts):
    n_x = n_c // 2
    rows, slots = form_blocks.shape[0], form_blocks.shape[2]
    size = emission.shape[0]
    cap = view_grads.shape[3]
    s = lax.axis_index("space")
    tall = slots * PK
    form = form_blocks.reshape(rows, slots, PK, 128).transpose(0, 2, 1, 3).reshape(rows, tall, 128)
    a, b = jnp.arange(tall)[:, None], jnp.arange(tall)[None, :]
    rows_perm = ((a % PK) * slots + a // PK == b).astype(BF16)
    q, p = jnp.arange(128)[:, None], jnp.arange(128)[None, :]
    lanes_perm = (q == (p // 64) * 64 + 2 * (p % 32) + (p % 64) // 32).astype(BF16)
    target = block_rows.reshape(rows, slots) - (s - 1) * rows
    block = target % rows
    piece = block // size
    target = target - block + ((piece % 2) * n_x + piece // 2) * size + block % size
    index = target.reshape(n_x, 2, size, slots).transpose(1, 0, 2, 3).reshape(rows * slots)
    col = lax.axis_index("col")
    lists = n_c * n_s
    at = ((col % 2) * n_x + col // 2) * n_s + s
    live = jnp.arange(cap, dtype=jnp.int32) < view_counts[0, 0][:, None]
    marks = jnp.where(live, view_rows[0, 0] + 1, 0)[:, None, :]
    own_list = jnp.arange(lists, dtype=jnp.int32)[None, :, None] == at
    meta = jnp.where(own_list, marks, 0).reshape(n_s, lists * cap)
    meta = jnp.pad(meta, ((0, 0), (0, -(lists * cap) % 128)))[:, None, :]

    dma = pltpu.SemaphoreType.DMA
    blocks = lambda n: (n, PK, 128)
    src, fwd_form, adj_form, gain, view_total, vector = call(
        functools.partial(start_kernel, n_x, n_s),
        [
            (blocks(rows), BF16),
            ((rows, tall, 128), BF16),
            ((rows, 128, tall), BF16),
            (blocks(size), F32),
            (blocks(size), F32),
            (blocks(3 * rows), BF16),
        ],
        [
            pltpu.VMEM(emission.shape, BF16),
            pltpu.VMEM(form.shape, BF16),
            pltpu.VMEM((lists, cap, BLK * CONF), BF16),
            pltpu.VMEM((lists,) + meta.shape[1:], jnp.int32),
            pltpu.VMEM((lists * cap, BLK * CONF), F32),
            pltpu.VMEM(blocks(size), F32),
        ]
        + [dma((2 * n_s + 12 * n_x,))] * 2 + [dma((4,))],
        (emission, view_grads[0, 0], form, reflect.reshape(-1, 128), meta, rows_perm, lanes_perm),
        hbm=3,
        vmem_bytes=FIRST_BYTES,
        remote=0,
    )
    group = n_x * size

    def forward(sources):
        return call(
            functools.partial(forward_local, slots),
            [(blocks(3 * rows), BF16)],
            [pltpu.VMEM(blocks(3 * rows), F32)],
            (index, fwd_form, sources),
            smem=1,
        )[0]

    bufs = [
        pltpu.VMEM(blocks(3 * group), BF16),
        pltpu.VMEM((2,) + blocks(group), BF16),
        pltpu.VMEM((2,) + blocks(group), BF16),
        pltpu.VMEM((n_x - 1,) + blocks(size), F32),
        pltpu.VMEM((n_x - 1,) + blocks(size), F32),
        pltpu.VMEM(blocks(rows), F32),
        pltpu.VMEM(blocks(group), F32),
        pltpu.VMEM((n_x - 1,) + blocks(size), F32),
        pltpu.VMEM((n_x - 1,) + blocks(size), F32),
    ]
    first_sums, bounced, adjoint_one, next_vector = call(
        functools.partial(middle_kernel, slots, n_x, n_s),
        [
            (blocks(size), F32),
            (blocks(rows), BF16),
            (blocks(size), F32),
            (blocks(3 * rows), BF16),
        ],
        bufs + [dma((16 * n_x,))] * 2,
        (index, forward(src), src, gain, vector, adj_form),
        smem=1,
        remote=1,
    )
    grad_emission, grad_reflect = call(
        functools.partial(end_kernel, slots, n_x, n_s),
        [((size, BLK * CONF), F32), ((size // 2, 128), F32)],
        bufs + [dma((8 * n_x,))] * 2,
        (index, forward(bounced), next_vector, adj_form, first_sums, adjoint_one, view_total),
        smem=1,
        remote=2,
    )
    return grad_emission, grad_reflect.reshape(size * BLK)


def solution(mesh):
    in_specs = (
        P(("level", "space", "col"), None),
        P(("level", "space", "col")),
        P(("level", "space"), "col", None, None),
        P(("level", "space"), "col", None),
        P(("level", "space"), "col", None, None, None),
        P(("level", "space"), "col", None, None),
        P(("level", "space"), "col", None),
    )
    out_specs = (P(("level", "space", "col"), None), P(("level", "space", "col")))
    step = functools.partial(body, mesh.shape["space"], mesh.shape["col"])
    return jax.shard_map(step, mesh=mesh, in_specs=in_specs, out_specs=out_specs, check_vma=False)
```

```python
import functools

import jax
import jax.numpy as jnp
from jax import lax
from jax.experimental import pallas as pl
from jax.experimental.pallas import tpu as pltpu
from jax.sharding import PartitionSpec as P

BLK = 64
CONF = 64
PK = BLK * CONF // 128
MESH = pl.DeviceIdType.MESH
F32 = jnp.float32
BF16 = jnp.bfloat16
VMEM_BYTES = 32 * 1024 * 1024
FIRST_BYTES = 48 * 1024 * 1024


class Net:
    def __init__(self, send_sems, recv_sems):
        self.send_sems, self.recv_sems, self.used = send_sems, recv_sems, 0

    def copy(self, src, dst, target):
        n = self.used
        self.used += 1
        return pltpu.make_async_remote_copy(
            src_ref=src,
            dst_ref=dst,
            send_sem=self.send_sems.at[n],
            recv_sem=self.recv_sems.at[n],
            device_id=target,
            device_id_type=MESH,
        )


def place():
    col = lax.axis_index("col")
    return lax.axis_index("space"), col // 2, col % 2


def greet(n_x, z_all, n_s):
    s, x, core = place()
    barrier = pltpu.get_barrier_semaphore()
    targets = [{"col": 2 * x + 1 - core}]
    targets += [{"col": 2 * ((x + d) % n_x) + core} for d in range(1, n_x)]
    if z_all:
        targets += [{"space": (s + d) % n_s} for d in range(1, n_s)]
    for target in targets:
        pl.semaphore_signal(barrier, inc=1, device_id=target, device_id_type=MESH)
    if not z_all:

        @pl.when(s > 0)
        def _():
            pl.semaphore_signal(barrier, inc=1, device_id={"space": s - 1}, device_id_type=MESH)

        @pl.when(s < n_s - 1)
        def _():
            pl.semaphore_signal(barrier, inc=1, device_id={"space": s + 1}, device_id_type=MESH)

    if z_all:
        pl.semaphore_wait(barrier, len(targets))
    else:
        sides = (s > 0).astype(jnp.int32) + (s < n_s - 1).astype(jnp.int32)
        pl.semaphore_wait(barrier, len(targets) + sides)


def low_half(rows):
    return lax.broadcasted_iota(jnp.int32, (rows, 128), 1) < 64


class GatherCol:
    def __init__(self, net, buf, n_x, size, base=0):
        s, x, core = place()
        self.net, self.buf, self.n_x, self.size, self.base = net, buf, n_x, size, base
        self.x, self.core = x, core
        mine = self.piece(core, x)
        self.across = []
        for d in range(1, n_x):
            self.across.append(net.copy(mine, mine, {"col": 2 * ((x + d) % n_x) + core}))
        self.beside = [net.copy(mine, mine, {"col": 2 * x + 1 - core})]
        for cp in self.across + self.beside:
            cp.start()

    def piece(self, core, x):
        return self.buf.at[pl.ds(self.base + (core * self.n_x + x) * self.size, self.size)]

    def arrive_across(self):
        for d, cp in enumerate(self.across, 1):
            cp.wait_recv()
            got = self.piece(self.core, (self.x + self.n_x - d) % self.n_x)
            on = self.net.copy(got, got, {"col": 2 * self.x + 1 - self.core})
            on.start()
            self.beside.append(on)

    def finish(self):
        for cp in self.beside:
            cp.wait_recv()
        for cp in self.beside + self.across:
            cp.wait_send()


class GatherWindow:
    def __init__(self, net, buf, n_x, size, n_s):
        s, x, core = place()
        self.net, self.buf, self.n_x, self.size, self.n_s = net, buf, n_x, size, n_s
        self.x, self.core = x, core
        self.z, self.beside = [], []
        self.across = []
        mine = self.piece(1, x)
        for d in range(1, n_x):
            cp = net.copy(mine, mine, {"col": 2 * ((x + d) % n_x) + core})
            cp.start()
            self.across.append(cp)
        self.along(x)
        self.pass_on(mine)

    def piece(self, run, x):
        start = ((2 * run + self.core) * self.n_x + x) * self.size
        return self.buf.at[pl.ds(start, self.size)]

    def pass_on(self, piece):
        cp = self.net.copy(piece, piece, {"col": 2 * self.x + 1 - self.core})
        cp.start()
        self.beside.append(cp)

    def along(self, x):
        s = lax.axis_index("space")
        up = self.net.copy(self.piece(1, x), self.piece(0, x), {"space": s + 1})
        down = self.net.copy(self.piece(1, x), self.piece(2, x), {"space": s - 1})
        pl.when(s < self.n_s - 1)(up.start)
        pl.when(s > 0)(down.start)
        self.z.append((up, down, x))

    def arrive_across(self):
        for d, cp in enumerate(self.across, 1):
            cp.wait_recv()
            at = (self.x + self.n_x - d) % self.n_x
            self.along(at)
            self.pass_on(self.piece(1, at))

    def finish(self):
        s = lax.axis_index("space")
        below, above = s > 0, s < self.n_s - 1
        other = {"col": 2 * self.x + 1 - self.core}
        for up, down, x in self.z:
            before = self.net.copy(self.piece(0, x), self.piece(0, x), other)
            after = self.net.copy(self.piece(2, x), self.piece(2, x), other)
            for there, came, on in ((below, up, before), (above, down, after)):

                @pl.when(there)
                def _(came=came, on=on):
                    came.wait_recv()
                    on.start()

            pl.when(above)(up.wait_send)
            pl.when(below)(down.wait_send)
            self.beside.append((below, before))
            self.beside.append((above, after))
        for cp in self.beside:
            if isinstance(cp, tuple):
                pl.when(cp[0])(cp[1].wait)
            else:
                cp.wait()
        for cp in self.across:
            cp.wait_send()


class SumForward:
    def __init__(self, net, part, got_core, z_out, z_in, x_out, x_in, n_x, size, n_s):
        s, x, core = place()
        self.net, self.part, self.got_core = net, part, got_core
        self.z_out, self.z_in, self.x_out, self.x_in = z_out, z_in, x_out, x_in
        self.n_x, self.size, self.n_s = n_x, size, n_s
        self.order = [(x + d) % n_x for d in list(range(1, n_x)) + [0]]
        self.first, self.z = {}, []
        for d, to in enumerate(self.order):
            for r in (0, 2, 1):
                src = part.at[pl.ds(((2 * r + 1 - core) * n_x + to) * size, size)]
                dst = got_core.at[pl.ds((r * n_x + to) * size, size)]
                cp = net.copy(src, dst, {"col": 2 * x + 1 - core})
                cp.start()
                self.first[d, r] = cp

    def pair(self, r, at):
        s, x, core = place()
        n_x, size = self.n_x, self.size
        mine = self.part[pl.ds(((2 * r + core) * n_x + at) * size, size)]
        return mine.astype(F32) + self.got_core[pl.ds((r * n_x + at) * size, size)].astype(F32)

    def along(self):
        s, x, core = place()
        for side, edge in ((0, s == 0), (1, s == self.n_s - 1)):

            @pl.when(edge)
            def _(side=side):
                self.z_in[side] = jnp.zeros(self.z_in.shape[1:], BF16)

        for d, to in enumerate(self.order):
            rows = pl.ds(to * self.size, self.size)
            down = self.net.copy(self.z_out.at[0, rows], self.z_in.at[1, rows], {"space": s - 1})
            up = self.net.copy(self.z_out.at[1, rows], self.z_in.at[0, rows], {"space": s + 1})
            self.first[d, 0].wait_recv()

            @pl.when(s > 0)
            def _(down=down, rows=rows, to=to):
                self.z_out[0, rows] = self.pair(0, to).astype(BF16)
                down.start()

            self.first[d, 2].wait_recv()

            @pl.when(s < self.n_s - 1)
            def _(up=up, rows=rows, to=to):
                self.z_out[1, rows] = self.pair(2, to).astype(BF16)
                up.start()

            self.z.append((down, up))

    def rows(self, d):
        s, x, core = place()
        self.first[d, 1].wait_recv()
        down, up = self.z[d]
        pl.when(s > 0)(up.wait_recv)
        pl.when(s < self.n_s - 1)(down.wait_recv)
        at = self.order[d]
        total = self.pair(1, at)
        for side in range(2):
            total = total + self.z_in[side, pl.ds(at * self.size, self.size)].astype(F32)
        return total

    def across(self):
        s, x, core = place()
        self.x = []
        for d in range(self.n_x - 1):
            self.x_out[d] = self.rows(d)
            to = {"col": 2 * self.order[d] + core}
            cp = self.net.copy(self.x_out.at[d], self.x_in.at[d], to)
            cp.start()
            self.x.append(cp)

    def finish(self):
        s, x, core = place()
        total = self.rows(self.n_x - 1)
        for d in range(self.n_x - 1):
            self.x[d].wait_recv()
            total = total + self.x_in[d]
        for cp in list(self.first.values()) + self.x:
            cp.wait_send()
        for down, up in self.z:
            pl.when(s > 0)(down.wait_send)
            pl.when(s < self.n_s - 1)(up.wait_send)
        return total


class SumCol:
    def __init__(self, net, part, got_core, x_out, x_in, n_x, size):
        s, x, core = place()
        self.net, self.part, self.got_core = net, part, got_core
        self.x_out, self.x_in, self.n_x, self.size = x_out, x_in, n_x, size
        self.group = n_x * size
        self.net = net
        self.first, self.x = [], []

    def beside(self, to):
        s, x, core = place()
        src = self.part.at[pl.ds((1 - core) * self.group + to * self.size, self.size)]
        dst = self.got_core.at[pl.ds(to * self.size, self.size)]
        cp = self.net.copy(src, dst, {"col": 2 * x + 1 - core})
        cp.start()
        self.first.append(cp)

    def rows(self, at):
        s, x, core = place()
        mine = self.part[pl.ds(core * self.group + at * self.size, self.size)]
        return mine + self.got_core[pl.ds(at * self.size, self.size)]

    def across(self):
        s, x, core = place()
        for d in range(1, self.n_x):
            to = (x + d) % self.n_x
            self.first[d - 1].wait_recv()
            self.x_out[d - 1] = self.rows(to)
            cp = self.net.copy(self.x_out.at[d - 1], self.x_in.at[d - 1], {"col": 2 * to + core})
            cp.start()
            self.x.append(cp)

    def finish(self):
        s, x, core = place()
        self.first[-1].wait_recv()
        total = self.rows(x)
        for d in range(1, self.n_x):
            self.x[d - 1].wait_recv()
            total = total + self.x_in[d - 1]
        for cp in self.first + self.x:
            cp.wait_send()
        return total


def patch_masks(p):
    i = lax.broadcasted_iota(jnp.int32, (PK, 128), 0)
    t = lax.broadcasted_iota(jnp.int32, (PK, 128), 1)
    rows = t == (p % 2) * 64 + 2 * i + t % 2
    patch = lax.broadcasted_iota(jnp.int32, (128, 128), 0)
    lane = lax.broadcasted_iota(jnp.int32, (128, 128), 1)
    return rows, (patch % 2 == lane // 64).astype(F32)


def start_kernel(
    n_x, n_s, emission_in, view, form_in, reflect, meta, rows_perm, lanes_perm,
    src, fwd_form, adj_form, gain, view_total, vector,
    emission, form, views, metas, entries, unpacked, send_sems, recv_sems, local_sem,
):
    s, x, core = place()
    size = emission.shape[0]
    cap = view.shape[1]
    rows = form.shape[0]
    net = Net(send_sems, recv_sems)
    where = core * n_x + x
    bring = pltpu.make_async_copy(emission_in, emission, local_sem.at[2])
    bring.start()
    bring_form = pltpu.make_async_copy(form_in, form, local_sem.at[3])
    bring_form.start()
    greet(n_x, True, n_s)
    at = where * n_s + s
    spread = []
    for d in range(1, n_s):
        to = (s + d) % n_s
        spread.append(net.copy(view.at[to], views.at[at], {"space": to}))
        spread.append(net.copy(meta.at[to], metas.at[at], {"space": to}))
    for cp in spread:
        cp.start()
    bring.wait()
    for i in range(PK):
        unpacked[:, i, :] = emission[:, i * 128 : (i + 1) * 128].astype(F32)
    src[pl.ds(where * size, size)] = unpacked[...].astype(BF16)
    own_view = pltpu.make_async_copy(view.at[s], views.at[at], local_sem.at[0])
    own_view.start()
    own_meta = pltpu.make_async_copy(meta.at[s], metas.at[at], local_sem.at[1])
    own_meta.start()
    gather = GatherCol(net, src, n_x, size)

    def prepare(t):
        j = t * 8
        c, r = j // size, j % size
        to = ((c % 2) * n_x + c // 2) * size + r
        plain = [
            jnp.dot(rows_perm[...], form[j + u], preferred_element_type=F32).astype(BF16)
            for u in range(8)
        ]
        tall = jnp.concatenate(plain, axis=0)
        turned = jnp.dot(tall, lanes_perm[...], preferred_element_type=F32).astype(BF16)
        for u in range(8):
            fwd_form[to + u] = turned[u * tall.shape[0] // 8 : (u + 1) * tall.shape[0] // 8]
            adj_form[to + u] = lax.dot_general(
                lanes_perm[...], plain[u], (((0,), (1,)), ((), ())), preferred_element_type=F32
            ).astype(BF16)

    eighth = rows // 8
    bring_form.wait()
    loop(0, eighth // 4, prepare, 1)
    own_view.wait()
    own_meta.wait()
    for cp in spread:
        cp.wait_recv()
    more = [GatherCol(net, views, n_x, n_s), GatherCol(net, metas, n_x, n_s)]
    gather.arrive_across()
    picked = []
    for p in range(size):
        sel, lanes = patch_masks(p)
        picked.append(jnp.where(sel, reflect[p // 2 : p // 2 + 1, :], 0.0))
    gain[...] = jnp.dot(
        jnp.concatenate(picked, axis=0), lanes,
        preferred_element_type=F32, precision=lax.Precision.HIGHEST,
    ).reshape(gain.shape)
    loop(eighth // 4, eighth // 4, prepare, 1)
    for g in more:
        g.arrive_across()
    gather.finish()
    for g in more:
        g.finish()
    count = views.shape[0] * cap
    for t in range(views.shape[0]):
        entries[t * cap : (t + 1) * cap, :] = views[t].astype(F32)
    marks = jnp.sum(metas[...], axis=0)
    wanted = lax.broadcasted_iota(jnp.int32, (size, marks.shape[1]), 0) + (2 * x + core) * size + 1
    chosen = (wanted == marks).astype(F32).astype(BF16)[:, :count]
    for i in range(0, PK, 4):
        cut = entries[:, i * 128 : (i + 4) * 128].astype(BF16)
        found = jnp.dot(chosen, cut, preferred_element_type=F32)
        for u in range(4):
            view_total[:, i + u, :] = found[:, u * 128 : (u + 1) * 128]
    vector[pl.ds(2 * n_x * size + where * size, size)] = (gain[...] * view_total[...]).astype(BF16)
    window = GatherWindow(net, vector, n_x, size, n_s)
    loop(eighth // 2, eighth // 4, prepare, 1)
    window.arrive_across()
    loop(eighth // 2 + eighth // 4, eighth // 4, prepare, 1)
    window.finish()
    for cp in spread:
        cp.wait_send()


def forward_step(j, form, src, index, slots, window):
    low = low_half(PK)
    piece = src[j].astype(F32)
    turned = pltpu.roll(piece, 64, 1)
    zero = jnp.zeros_like(piece)
    wide = jnp.concatenate(
        [
            jnp.where(low, piece, zero),
            jnp.where(low, turned, zero),
            jnp.where(low, zero, turned),
            jnp.where(low, zero, piece),
        ],
        axis=0,
    ).astype(BF16)
    terms = jnp.dot(form[j], wide, preferred_element_type=F32)
    for k in range(slots):
        at = index[j * slots + k]
        window[at] = window[at] + terms[k * PK : (k + 1) * PK]


def adjoint_step(j, form, vector, index, slots, out):
    low = low_half(PK)
    picked = jnp.concatenate([vector[index[j * slots + k]] for k in range(slots)], axis=0)
    m = jnp.dot(form[j], picked, preferred_element_type=F32)
    even = m[:PK] + pltpu.roll(m[2 * PK : 3 * PK], 64, 1)
    odd = pltpu.roll(m[PK : 2 * PK], 64, 1) + m[3 * PK :]
    out[j] = jnp.where(low, even, odd)


def loop(first, count, step, unroll):
    def body(t, carry):
        for u in range(unroll):
            step(first + t * unroll + u)
        return carry

    lax.fori_loop(0, count // unroll, body, 0)


def clear(window):
    def body(t, carry):
        window[pl.ds(t * 8, 8)] = jnp.zeros((8,) + window.shape[1:], F32)
        return carry

    lax.fori_loop(0, window.shape[0] // 8, body, 0)


def write_part(window, part):
    def body(t, carry):
        part[pl.ds(t * 8, 8)] = window[pl.ds(t * 8, 8)].astype(BF16)
        return carry

    lax.fori_loop(0, window.shape[0] // 8, body, 0)


def forward_local(slots, index, form, src, part, window):
    clear(window)
    loop(0, form.shape[0], lambda j: forward_step(j, form, src, index, slots, window), 8)
    write_part(window, part)


def adjoint_beside(col_sum, sums, step, n_x, size):
    s, x, core = place()
    others = [(x + d) % n_x for d in range(1, n_x)]
    for to in others:
        loop(((1 - core) * n_x + to) * size, size, step, 8)
        col_sum.beside(to)
    sums.along()
    for to in others:
        loop((core * n_x + to) * size, size, step, 8)
    col_sum.across()
    loop(((1 - core) * n_x + x) * size, size, step, 8)
    col_sum.beside(x)
    loop((core * n_x + x) * size, size, step, 8)


def middle_kernel(
    slots, n_x, n_s, index, part, src, gain, vector, adj_form,
    first_sums, bounced, adjoint_one, next_vector,
    got_core, z_out, z_in, x_out, x_in,
    terms, one_core, one_out, one_in, send_sems, recv_sems,
):
    s, x, core = place()
    size = gain.shape[0]
    net = Net(send_sems, recv_sems)
    greet(n_x, False, n_s)
    mine = (core * n_x + x) * size
    group = n_x * size
    step = lambda j: adjoint_step(j, adj_form, vector, index, slots, terms)
    sums = SumForward(net, part, got_core, z_out, z_in, x_out, x_in, n_x, size, n_s)
    one = SumCol(net, terms, one_core, one_out, one_in, n_x, size)
    adjoint_beside(one, sums, step, n_x, size)
    sums.across()
    adjoint_one[...] = one.finish()
    next_vector[pl.ds(2 * group + mine, size)] = (gain[...] * adjoint_one[...]).astype(BF16)
    gather = GatherWindow(net, next_vector, n_x, size, n_s)
    first_sums[...] = sums.finish()
    bounced[pl.ds(mine, size)] = (
        src[pl.ds(mine, size)].astype(F32) + gain[...] * first_sums[...]
    ).astype(BF16)
    second = GatherCol(net, bounced, n_x, size)
    gather.arrive_across()
    second.arrive_across()
    gather.finish()
    second.finish()


def end_kernel(
    slots, n_x, n_s, index, part, vector, adj_form, first_sums, adjoint_one, view_total,
    grad_emission, grad_reflect,
    got_core, z_out, z_in, x_out, x_in,
    terms, two_core, two_out, two_in, send_sems, recv_sems,
):
    s, x, core = place()
    size = view_total.shape[0]
    net = Net(send_sems, recv_sems)
    greet(n_x, False, n_s)
    group = n_x * size
    step = lambda j: adjoint_step(j, adj_form, vector, index, slots, terms)
    sums = SumForward(net, part, got_core, z_out, z_in, x_out, x_in, n_x, size, n_s)
    two = SumCol(net, terms, two_core, two_out, two_in, n_x, size)
    adjoint_beside(two, sums, step, n_x, size)
    sums.across()
    got_two = two.finish()
    keep = two_core
    keep[pl.ds(0, size)] = view_total[...] + adjoint_one[...] + got_two
    for i in range(PK):
        grad_emission[:, i * 128 : (i + 1) * 128] = keep[:size, i, :]
    product = view_total[...] * sums.finish() + adjoint_one[...] * first_sums[...]
    lanes = patch_masks(0)[1]
    halves = lax.dot_general(
        product.reshape(size * PK, 128), lanes, (((1,), (1,)), ((), ())),
        preferred_element_type=F32, precision=lax.Precision.HIGHEST,
    )
    for p in range(0, size, 2):
        total = jnp.zeros((1, 128), F32)
        for q in (p, p + 1):
            sel = patch_masks(q)[0]
            part_q = jnp.where(sel, halves[q * PK : (q + 1) * PK], 0.0)
            total = total + jnp.sum(part_q, axis=0, keepdims=True)
        grad_reflect[p // 2 : p // 2 + 1, :] = total


def call(kernel, outs, scratch, operands, smem=0, hbm=0, remote=None, vmem_bytes=VMEM_BYTES):
    vmem = pl.BlockSpec(memory_space=pltpu.VMEM)
    specs = [pl.BlockSpec(memory_space=pltpu.SMEM)] * smem
    specs += [pl.BlockSpec(memory_space=pltpu.HBM)] * hbm
    specs += [vmem] * (len(operands) - smem - hbm)
    if remote is None:
        params = pltpu.CompilerParams(vmem_limit_bytes=vmem_bytes)
    else:
        params = pltpu.CompilerParams(
            vmem_limit_bytes=vmem_bytes, collective_id=remote, has_side_effects=True
        )
    return pl.pallas_call(
        kernel,
        out_shape=[jax.ShapeDtypeStruct(*out) for out in outs],
        in_specs=specs,
        out_specs=[vmem] * len(outs),
        scratch_shapes=scratch,
        compiler_params=params,
    )(*operands)


def body(n_s, n_c, emission, reflect, form_blocks, block_rows, view_grads, view_rows, view_counts):
    n_x = n_c // 2
    rows, slots = form_blocks.shape[0], form_blocks.shape[2]
    size = emission.shape[0]
    cap = view_grads.shape[3]
    s = lax.axis_index("space")
    tall = slots * PK
    form = form_blocks.reshape(rows, slots, PK, 128).transpose(0, 2, 1, 3).reshape(rows, tall, 128)
    a, b = jnp.arange(tall)[:, None], jnp.arange(tall)[None, :]
    rows_perm = ((a % PK) * slots + a // PK == b).astype(BF16)
    q, p = jnp.arange(128)[:, None], jnp.arange(128)[None, :]
    lanes_perm = (q == (p // 64) * 64 + 2 * (p % 32) + (p % 64) // 32).astype(BF16)
    target = block_rows.reshape(rows, slots) - (s - 1) * rows
    block = target % rows
    piece = block // size
    target = target - block + ((piece % 2) * n_x + piece // 2) * size + block % size
    index = target.reshape(n_x, 2, size, slots).transpose(1, 0, 2, 3).reshape(rows * slots)
    col = lax.axis_index("col")
    lists = n_c * n_s
    at = ((col % 2) * n_x + col // 2) * n_s + s
    live = jnp.arange(cap, dtype=jnp.int32) < view_counts[0, 0][:, None]
    marks = jnp.where(live, view_rows[0, 0] + 1, 0)[:, None, :]
    own_list = jnp.arange(lists, dtype=jnp.int32)[None, :, None] == at
    meta = jnp.where(own_list, marks, 0).reshape(n_s, lists * cap)
    meta = jnp.pad(meta, ((0, 0), (0, -(lists * cap) % 128)))[:, None, :]

    dma = pltpu.SemaphoreType.DMA
    blocks = lambda n: (n, PK, 128)
    src, fwd_form, adj_form, gain, view_total, vector = call(
        functools.partial(start_kernel, n_x, n_s),
        [
            (blocks(rows), BF16),
            ((rows, tall, 128), BF16),
            ((rows, 128, tall), BF16),
            (blocks(size), F32),
            (blocks(size), F32),
            (blocks(3 * rows), BF16),
        ],
        [
            pltpu.VMEM(emission.shape, BF16),
            pltpu.VMEM(form.shape, BF16),
            pltpu.VMEM((lists, cap, BLK * CONF), BF16),
            pltpu.VMEM((lists,) + meta.shape[1:], jnp.int32),
            pltpu.VMEM((lists * cap, BLK * CONF), F32),
            pltpu.VMEM(blocks(size), F32),
        ]
        + [dma((2 * n_s + 12 * n_x,))] * 2 + [dma((4,))],
        (emission, view_grads[0, 0], form, reflect.reshape(-1, 128), meta, rows_perm, lanes_perm),
        hbm=3,
        vmem_bytes=FIRST_BYTES,
        remote=0,
    )
    group = n_x * size

    def forward(sources):
        return call(
            functools.partial(forward_local, slots),
            [(blocks(3 * rows), BF16)],
            [pltpu.VMEM(blocks(3 * rows), F32)],
            (index, fwd_form, sources),
            smem=1,
        )[0]

    bufs = [
        pltpu.VMEM(blocks(3 * group), BF16),
        pltpu.VMEM((2,) + blocks(group), BF16),
        pltpu.VMEM((2,) + blocks(group), BF16),
        pltpu.VMEM((n_x - 1,) + blocks(size), F32),
        pltpu.VMEM((n_x - 1,) + blocks(size), F32),
        pltpu.VMEM(blocks(rows), F32),
        pltpu.VMEM(blocks(group), F32),
        pltpu.VMEM((n_x - 1,) + blocks(size), F32),
        pltpu.VMEM((n_x - 1,) + blocks(size), F32),
    ]
    first_sums, bounced, adjoint_one, next_vector = call(
        functools.partial(middle_kernel, slots, n_x, n_s),
        [
            (blocks(size), F32),
            (blocks(rows), BF16),
            (blocks(size), F32),
            (blocks(3 * rows), BF16),
        ],
        bufs + [dma((16 * n_x,))] * 2,
        (index, forward(src), src, gain, vector, adj_form),
        smem=1,
        remote=1,
    )
    grad_emission, grad_reflect = call(
        functools.partial(end_kernel, slots, n_x, n_s),
        [((size, BLK * CONF), F32), ((size // 2, 128), F32)],
        bufs + [dma((8 * n_x,))] * 2,
        (index, forward(bounced), next_vector, adj_form, first_sums, adjoint_one, view_total),
        smem=1,
        remote=2,
    )
    return grad_emission, grad_reflect.reshape(size * BLK)


def solution(mesh):
    in_specs = (
        P(("level", "space", "col"), None),
        P(("level", "space", "col")),
        P(("level", "space"), "col", None, None),
        P(("level", "space"), "col", None),
        P(("level", "space"), "col", None, None, None),
        P(("level", "space"), "col", None, None),
        P(("level", "space"), "col", None),
    )
    out_specs = (P(("level", "space", "col"), None), P(("level", "space", "col")))
    step = functools.partial(body, mesh.shape["space"], mesh.shape["col"])
    return jax.shard_map(step, mesh=mesh, in_specs=in_specs, out_specs=out_specs, check_vma=False)
```

```python
import functools

import jax
import jax.numpy as jnp
from jax import lax
from jax.experimental import pallas as pl
from jax.experimental.pallas import tpu as pltpu
from jax.sharding import PartitionSpec as P

BLK = 64
CONF = 64
PK = BLK * CONF // 128
MESH = pl.DeviceIdType.MESH
F32 = jnp.float32
BF16 = jnp.bfloat16
VMEM_BYTES = 32 * 1024 * 1024
FIRST_BYTES = 48 * 1024 * 1024


class Net:
    def __init__(self, send_sems, recv_sems):
        self.send_sems, self.recv_sems, self.used = send_sems, recv_sems, 0

    def copy(self, src, dst, target):
        n = self.used
        self.used += 1
        return pltpu.make_async_remote_copy(
            src_ref=src,
            dst_ref=dst,
            send_sem=self.send_sems.at[n],
            recv_sem=self.recv_sems.at[n],
            device_id=target,
            device_id_type=MESH,
        )


def place():
    col = lax.axis_index("col")
    return lax.axis_index("space"), col // 2, col % 2


def greet(n_x, z_all, n_s):
    s, x, core = place()
    barrier = pltpu.get_barrier_semaphore()
    targets = [{"col": 2 * x + 1 - core}]
    targets += [{"col": 2 * ((x + d) % n_x) + core} for d in range(1, n_x)]
    if z_all:
        targets += [{"space": (s + d) % n_s} for d in range(1, n_s)]
    for target in targets:
        pl.semaphore_signal(barrier, inc=1, device_id=target, device_id_type=MESH)
    if not z_all:

        @pl.when(s > 0)
        def _():
            pl.semaphore_signal(barrier, inc=1, device_id={"space": s - 1}, device_id_type=MESH)

        @pl.when(s < n_s - 1)
        def _():
            pl.semaphore_signal(barrier, inc=1, device_id={"space": s + 1}, device_id_type=MESH)

    if z_all:
        pl.semaphore_wait(barrier, len(targets))
    else:
        sides = (s > 0).astype(jnp.int32) + (s < n_s - 1).astype(jnp.int32)
        pl.semaphore_wait(barrier, len(targets) + sides)


def low_half(rows):
    return lax.broadcasted_iota(jnp.int32, (rows, 128), 1) < 64


class GatherCol:
    def __init__(self, net, buf, n_x, size, base=0):
        s, x, core = place()
        self.net, self.buf, self.n_x, self.size, self.base = net, buf, n_x, size, base
        self.x, self.core = x, core
        mine = self.piece(core, x)
        self.across = []
        for d in range(1, n_x):
            self.across.append(net.copy(mine, mine, {"col": 2 * ((x + d) % n_x) + core}))
        self.beside = [net.copy(mine, mine, {"col": 2 * x + 1 - core})]
        for cp in self.across + self.beside:
            cp.start()

    def piece(self, core, x):
        return self.buf.at[pl.ds(self.base + (core * self.n_x + x) * self.size, self.size)]

    def arrive_across(self):
        for d, cp in enumerate(self.across, 1):
            cp.wait_recv()
            got = self.piece(self.core, (self.x + self.n_x - d) % self.n_x)
            on = self.net.copy(got, got, {"col": 2 * self.x + 1 - self.core})
            on.start()
            self.beside.append(on)

    def finish(self):
        for cp in self.beside:
            cp.wait_recv()
        for cp in self.beside + self.across:
            cp.wait_send()


class GatherWindow:
    def __init__(self, net, buf, n_x, size, n_s):
        s, x, core = place()
        self.net, self.buf, self.n_x, self.size, self.n_s = net, buf, n_x, size, n_s
        self.x, self.core = x, core
        self.z, self.beside = [], []
        self.across = []
        mine = self.piece(1, x)
        for d in range(1, n_x):
            cp = net.copy(mine, mine, {"col": 2 * ((x + d) % n_x) + core})
            cp.start()
            self.across.append(cp)
        self.along(x)
        self.pass_on(mine)

    def piece(self, run, x):
        start = ((2 * run + self.core) * self.n_x + x) * self.size
        return self.buf.at[pl.ds(start, self.size)]

    def pass_on(self, piece):
        cp = self.net.copy(piece, piece, {"col": 2 * self.x + 1 - self.core})
        cp.start()
        self.beside.append(cp)

    def along(self, x):
        s = lax.axis_index("space")
        up = self.net.copy(self.piece(1, x), self.piece(0, x), {"space": s + 1})
        down = self.net.copy(self.piece(1, x), self.piece(2, x), {"space": s - 1})
        pl.when(s < self.n_s - 1)(up.start)
        pl.when(s > 0)(down.start)
        self.z.append((up, down, x))

    def arrive_across(self):
        for d, cp in enumerate(self.across, 1):
            cp.wait_recv()
            at = (self.x + self.n_x - d) % self.n_x
            self.along(at)
            self.pass_on(self.piece(1, at))

    def finish(self):
        s = lax.axis_index("space")
        below, above = s > 0, s < self.n_s - 1
        other = {"col": 2 * self.x + 1 - self.core}
        for up, down, x in self.z:
            before = self.net.copy(self.piece(0, x), self.piece(0, x), other)
            after = self.net.copy(self.piece(2, x), self.piece(2, x), other)
            for there, came, on in ((below, up, before), (above, down, after)):

                @pl.when(there)
                def _(came=came, on=on):
                    came.wait_recv()
                    on.start()

            pl.when(above)(up.wait_send)
            pl.when(below)(down.wait_send)
            self.beside.append((below, before))
            self.beside.append((above, after))
        for cp in self.beside:
            if isinstance(cp, tuple):
                pl.when(cp[0])(cp[1].wait)
            else:
                cp.wait()
        for cp in self.across:
            cp.wait_send()


class SumForward:
    def __init__(self, net, part, got_core, z_out, z_in, x_out, x_in, n_x, size, n_s):
        s, x, core = place()
        self.net, self.part, self.got_core = net, part, got_core
        self.z_out, self.z_in, self.x_out, self.x_in = z_out, z_in, x_out, x_in
        self.n_x, self.size, self.n_s = n_x, size, n_s
        self.order = [(x + d) % n_x for d in list(range(1, n_x)) + [0]]
        self.first, self.z = {}, []
        for d, to in enumerate(self.order):
            for r in (0, 2, 1):
                src = part.at[pl.ds(((2 * r + 1 - core) * n_x + to) * size, size)]
                dst = got_core.at[pl.ds((r * n_x + to) * size, size)]
                cp = net.copy(src, dst, {"col": 2 * x + 1 - core})
                cp.start()
                self.first[d, r] = cp

    def pair(self, r, at):
        s, x, core = place()
        n_x, size = self.n_x, self.size
        mine = self.part[pl.ds(((2 * r + core) * n_x + at) * size, size)]
        return mine.astype(F32) + self.got_core[pl.ds((r * n_x + at) * size, size)].astype(F32)

    def along(self):
        s, x, core = place()
        for side, edge in ((0, s == 0), (1, s == self.n_s - 1)):

            @pl.when(edge)
            def _(side=side):
                self.z_in[side] = jnp.zeros(self.z_in.shape[1:], BF16)

        for d, to in enumerate(self.order):
            rows = pl.ds(to * self.size, self.size)
            down = self.net.copy(self.z_out.at[0, rows], self.z_in.at[1, rows], {"space": s - 1})
            up = self.net.copy(self.z_out.at[1, rows], self.z_in.at[0, rows], {"space": s + 1})
            self.first[d, 0].wait_recv()

            @pl.when(s > 0)
            def _(down=down, rows=rows, to=to):
                self.z_out[0, rows] = self.pair(0, to).astype(BF16)
                down.start()

            self.first[d, 2].wait_recv()

            @pl.when(s < self.n_s - 1)
            def _(up=up, rows=rows, to=to):
                self.z_out[1, rows] = self.pair(2, to).astype(BF16)
                up.start()

            self.z.append((down, up))

    def rows(self, d):
        s, x, core = place()
        self.first[d, 1].wait_recv()
        down, up = self.z[d]
        pl.when(s > 0)(up.wait_recv)
        pl.when(s < self.n_s - 1)(down.wait_recv)
        at = self.order[d]
        total = self.pair(1, at)
        for side in range(2):
            total = total + self.z_in[side, pl.ds(at * self.size, self.size)].astype(F32)
        return total

    def across(self):
        s, x, core = place()
        self.x = []
        for d in range(self.n_x - 1):
            self.x_out[d] = self.rows(d)
            to = {"col": 2 * self.order[d] + core}
            cp = self.net.copy(self.x_out.at[d], self.x_in.at[d], to)
            cp.start()
            self.x.append(cp)

    def finish(self):
        s, x, core = place()
        total = self.rows(self.n_x - 1)
        for d in range(self.n_x - 1):
            self.x[d].wait_recv()
            total = total + self.x_in[d]
        for cp in list(self.first.values()) + self.x:
            cp.wait_send()
        for down, up in self.z:
            pl.when(s > 0)(down.wait_send)
            pl.when(s < self.n_s - 1)(up.wait_send)
        return total


class SumCol:
    def __init__(self, net, part, got_core, x_out, x_in, n_x, size):
        s, x, core = place()
        self.net, self.part, self.got_core = net, part, got_core
        self.x_out, self.x_in, self.n_x, self.size = x_out, x_in, n_x, size
        self.group = n_x * size
        self.net = net
        self.first, self.x = [], []

    def beside(self, to):
        s, x, core = place()
        src = self.part.at[pl.ds((1 - core) * self.group + to * self.size, self.size)]
        dst = self.got_core.at[pl.ds(to * self.size, self.size)]
        cp = self.net.copy(src, dst, {"col": 2 * x + 1 - core})
        cp.start()
        self.first.append(cp)

    def rows(self, at):
        s, x, core = place()
        mine = self.part[pl.ds(core * self.group + at * self.size, self.size)]
        return mine + self.got_core[pl.ds(at * self.size, self.size)]

    def across(self):
        s, x, core = place()
        for d in range(1, self.n_x):
            to = (x + d) % self.n_x
            self.first[d - 1].wait_recv()
            self.x_out[d - 1] = self.rows(to)
            cp = self.net.copy(self.x_out.at[d - 1], self.x_in.at[d - 1], {"col": 2 * to + core})
            cp.start()
            self.x.append(cp)

    def finish(self):
        s, x, core = place()
        self.first[-1].wait_recv()
        total = self.rows(x)
        for d in range(1, self.n_x):
            self.x[d - 1].wait_recv()
            total = total + self.x_in[d - 1]
        for cp in self.first + self.x:
            cp.wait_send()
        return total


def patch_masks(p):
    i = lax.broadcasted_iota(jnp.int32, (PK, 128), 0)
    t = lax.broadcasted_iota(jnp.int32, (PK, 128), 1)
    rows = t == (p % 2) * 64 + 2 * i + t % 2
    patch = lax.broadcasted_iota(jnp.int32, (128, 128), 0)
    lane = lax.broadcasted_iota(jnp.int32, (128, 128), 1)
    return rows, (patch % 2 == lane // 64).astype(F32)


def start_kernel(
    n_x, n_s, emission_in, view, form_in, reflect, meta, rows_perm, lanes_perm,
    src, fwd_form, adj_form, gain, view_total, vector,
    emission, form, views, metas, entries, unpacked, send_sems, recv_sems, local_sem,
):
    s, x, core = place()
    size = emission.shape[0]
    cap = view.shape[1]
    rows = form.shape[0]
    net = Net(send_sems, recv_sems)
    where = core * n_x + x
    bring = pltpu.make_async_copy(emission_in, emission, local_sem.at[2])
    bring.start()
    bring_form = pltpu.make_async_copy(form_in, form, local_sem.at[3])
    bring_form.start()
    greet(n_x, True, n_s)
    at = where * n_s + s
    spread = []
    for d in range(1, n_s):
        to = (s + d) % n_s
        spread.append(net.copy(view.at[to], views.at[at], {"space": to}))
        spread.append(net.copy(meta.at[to], metas.at[at], {"space": to}))
    for cp in spread:
        cp.start()
    bring.wait()
    for i in range(PK):
        unpacked[:, i, :] = emission[:, i * 128 : (i + 1) * 128].astype(F32)
    src[pl.ds(where * size, size)] = unpacked[...].astype(BF16)
    own_view = pltpu.make_async_copy(view.at[s], views.at[at], local_sem.at[0])
    own_view.start()
    own_meta = pltpu.make_async_copy(meta.at[s], metas.at[at], local_sem.at[1])
    own_meta.start()
    gather = GatherCol(net, src, n_x, size)

    def prepare(t):
        j = t * 8
        c, r = j // size, j % size
        to = ((c % 2) * n_x + c // 2) * size + r
        plain = [
            jnp.dot(rows_perm[...], form[j + u], preferred_element_type=F32).astype(BF16)
            for u in range(8)
        ]
        tall = jnp.concatenate(plain, axis=0)
        turned = jnp.dot(tall, lanes_perm[...], preferred_element_type=F32).astype(BF16)
        for u in range(8):
            fwd_form[to + u] = turned[u * tall.shape[0] // 8 : (u + 1) * tall.shape[0] // 8]
            adj_form[to + u] = lax.dot_general(
                lanes_perm[...], plain[u], (((0,), (1,)), ((), ())), preferred_element_type=F32
            ).astype(BF16)

    eighth = rows // 8
    bring_form.wait()
    loop(0, eighth // 4, prepare, 1)
    own_view.wait()
    own_meta.wait()
    for cp in spread:
        cp.wait_recv()
    more = [GatherCol(net, views, n_x, n_s), GatherCol(net, metas, n_x, n_s)]
    gather.arrive_across()
    picked = []
    for p in range(size):
        sel, lanes = patch_masks(p)
        picked.append(jnp.where(sel, reflect[p // 2 : p // 2 + 1, :], 0.0))
    gain[...] = jnp.dot(
        jnp.concatenate(picked, axis=0), lanes,
        preferred_element_type=F32, precision=lax.Precision.HIGHEST,
    ).reshape(gain.shape)
    loop(eighth // 4, eighth // 4, prepare, 1)
    for g in more:
        g.arrive_across()
    for g in more:
        g.finish()
    count = views.shape[0] * cap
    for t in range(views.shape[0]):
        entries[t * cap : (t + 1) * cap, :] = views[t].astype(F32)
    marks = jnp.sum(metas[...], axis=0)
    wanted = lax.broadcasted_iota(jnp.int32, (size, marks.shape[1]), 0) + (2 * x + core) * size + 1
    chosen = (wanted == marks).astype(F32).astype(BF16)[:, :count]
    for i in range(0, PK, 4):
        cut = entries[:, i * 128 : (i + 4) * 128].astype(BF16)
        found = jnp.dot(chosen, cut, preferred_element_type=F32)
        for u in range(4):
            view_total[:, i + u, :] = found[:, u * 128 : (u + 1) * 128]
    vector[pl.ds(2 * n_x * size + where * size, size)] = (gain[...] * view_total[...]).astype(BF16)
    window = GatherWindow(net, vector, n_x, size, n_s)
    loop(eighth // 2, eighth // 4, prepare, 1)
    window.arrive_across()
    loop(eighth // 2 + eighth // 4, eighth // 4, prepare, 1)
    window.finish()
    gather.finish()
    for cp in spread:
        cp.wait_send()


def forward_step(j, form, src, index, slots, window):
    low = low_half(PK)
    piece = src[j].astype(F32)
    turned = pltpu.roll(piece, 64, 1)
    zero = jnp.zeros_like(piece)
    wide = jnp.concatenate(
        [
            jnp.where(low, piece, zero),
            jnp.where(low, turned, zero),
            jnp.where(low, zero, turned),
            jnp.where(low, zero, piece),
        ],
        axis=0,
    ).astype(BF16)
    terms = jnp.dot(form[j], wide, preferred_element_type=F32)
    for k in range(slots):
        at = index[j * slots + k]
        window[at] = window[at] + terms[k * PK : (k + 1) * PK]


def adjoint_step(j, form, vector, index, slots, out):
    low = low_half(PK)
    picked = jnp.concatenate([vector[index[j * slots + k]] for k in range(slots)], axis=0)
    m = jnp.dot(form[j], picked, preferred_element_type=F32)
    even = m[:PK] + pltpu.roll(m[2 * PK : 3 * PK], 64, 1)
    odd = pltpu.roll(m[PK : 2 * PK], 64, 1) + m[3 * PK :]
    out[j] = jnp.where(low, even, odd)


def loop(first, count, step, unroll):
    def body(t, carry):
        for u in range(unroll):
            step(first + t * unroll + u)
        return carry

    lax.fori_loop(0, count // unroll, body, 0)


def clear(window):
    def body(t, carry):
        window[pl.ds(t * 8, 8)] = jnp.zeros((8,) + window.shape[1:], F32)
        return carry

    lax.fori_loop(0, window.shape[0] // 8, body, 0)


def write_part(window, part):
    def body(t, carry):
        part[pl.ds(t * 8, 8)] = window[pl.ds(t * 8, 8)].astype(BF16)
        return carry

    lax.fori_loop(0, window.shape[0] // 8, body, 0)


def forward_local(slots, index, form, src, part, window):
    clear(window)
    loop(0, form.shape[0], lambda j: forward_step(j, form, src, index, slots, window), 8)
    write_part(window, part)


def adjoint_beside(col_sum, sums, step, n_x, size):
    s, x, core = place()
    others = [(x + d) % n_x for d in range(1, n_x)]
    for to in others:
        loop(((1 - core) * n_x + to) * size, size, step, 8)
        col_sum.beside(to)
    sums.along()
    for to in others:
        loop((core * n_x + to) * size, size, step, 8)
    col_sum.across()
    loop(((1 - core) * n_x + x) * size, size, step, 8)
    col_sum.beside(x)
    loop((core * n_x + x) * size, size, step, 8)


def middle_kernel(
    slots, n_x, n_s, index, part, src, gain, vector, adj_form,
    first_sums, bounced, adjoint_one, next_vector,
    got_core, z_out, z_in, x_out, x_in,
    terms, one_core, one_out, one_in, send_sems, recv_sems,
):
    s, x, core = place()
    size = gain.shape[0]
    net = Net(send_sems, recv_sems)
    greet(n_x, False, n_s)
    mine = (core * n_x + x) * size
    group = n_x * size
    step = lambda j: adjoint_step(j, adj_form, vector, index, slots, terms)
    sums = SumForward(net, part, got_core, z_out, z_in, x_out, x_in, n_x, size, n_s)
    one = SumCol(net, terms, one_core, one_out, one_in, n_x, size)
    adjoint_beside(one, sums, step, n_x, size)
    sums.across()
    adjoint_one[...] = one.finish()
    next_vector[pl.ds(2 * group + mine, size)] = (gain[...] * adjoint_one[...]).astype(BF16)
    gather = GatherWindow(net, next_vector, n_x, size, n_s)
    first_sums[...] = sums.finish()
    bounced[pl.ds(mine, size)] = (
        src[pl.ds(mine, size)].astype(F32) + gain[...] * first_sums[...]
    ).astype(BF16)
    second = GatherCol(net, bounced, n_x, size)
    gather.arrive_across()
    second.arrive_across()
    gather.finish()
    second.finish()


def end_kernel(
    slots, n_x, n_s, index, part, vector, adj_form, first_sums, adjoint_one, view_total,
    grad_emission, grad_reflect,
    got_core, z_out, z_in, x_out, x_in,
    terms, two_core, two_out, two_in, send_sems, recv_sems,
):
    s, x, core = place()
    size = view_total.shape[0]
    net = Net(send_sems, recv_sems)
    greet(n_x, False, n_s)
    group = n_x * size
    step = lambda j: adjoint_step(j, adj_form, vector, index, slots, terms)
    sums = SumForward(net, part, got_core, z_out, z_in, x_out, x_in, n_x, size, n_s)
    two = SumCol(net, terms, two_core, two_out, two_in, n_x, size)
    adjoint_beside(two, sums, step, n_x, size)
    sums.across()
    got_two = two.finish()
    keep = two_core
    keep[pl.ds(0, size)] = view_total[...] + adjoint_one[...] + got_two
    for i in range(PK):
        grad_emission[:, i * 128 : (i + 1) * 128] = keep[:size, i, :]
    product = view_total[...] * sums.finish() + adjoint_one[...] * first_sums[...]
    lanes = patch_masks(0)[1]
    halves = lax.dot_general(
        product.reshape(size * PK, 128), lanes, (((1,), (1,)), ((), ())),
        preferred_element_type=F32, precision=lax.Precision.HIGHEST,
    )
    for p in range(0, size, 2):
        total = jnp.zeros((1, 128), F32)
        for q in (p, p + 1):
            sel = patch_masks(q)[0]
            part_q = jnp.where(sel, halves[q * PK : (q + 1) * PK], 0.0)
            total = total + jnp.sum(part_q, axis=0, keepdims=True)
        grad_reflect[p // 2 : p // 2 + 1, :] = total


def call(kernel, outs, scratch, operands, smem=0, hbm=0, remote=None, vmem_bytes=VMEM_BYTES):
    vmem = pl.BlockSpec(memory_space=pltpu.VMEM)
    specs = [pl.BlockSpec(memory_space=pltpu.SMEM)] * smem
    specs += [pl.BlockSpec(memory_space=pltpu.HBM)] * hbm
    specs += [vmem] * (len(operands) - smem - hbm)
    if remote is None:
        params = pltpu.CompilerParams(vmem_limit_bytes=vmem_bytes)
    else:
        params = pltpu.CompilerParams(
            vmem_limit_bytes=vmem_bytes, collective_id=remote, has_side_effects=True
        )
    return pl.pallas_call(
        kernel,
        out_shape=[jax.ShapeDtypeStruct(*out) for out in outs],
        in_specs=specs,
        out_specs=[vmem] * len(outs),
        scratch_shapes=scratch,
        compiler_params=params,
    )(*operands)


def body(n_s, n_c, emission, reflect, form_blocks, block_rows, view_grads, view_rows, view_counts):
    n_x = n_c // 2
    rows, slots = form_blocks.shape[0], form_blocks.shape[2]
    size = emission.shape[0]
    cap = view_grads.shape[3]
    s = lax.axis_index("space")
    tall = slots * PK
    form = form_blocks.reshape(rows, slots, PK, 128).transpose(0, 2, 1, 3).reshape(rows, tall, 128)
    a, b = jnp.arange(tall)[:, None], jnp.arange(tall)[None, :]
    rows_perm = ((a % PK) * slots + a // PK == b).astype(BF16)
    q, p = jnp.arange(128)[:, None], jnp.arange(128)[None, :]
    lanes_perm = (q == (p // 64) * 64 + 2 * (p % 32) + (p % 64) // 32).astype(BF16)
    target = block_rows.reshape(rows, slots) - (s - 1) * rows
    block = target % rows
    piece = block // size
    target = target - block + ((piece % 2) * n_x + piece // 2) * size + block % size
    index = target.reshape(n_x, 2, size, slots).transpose(1, 0, 2, 3).reshape(rows * slots)
    col = lax.axis_index("col")
    lists = n_c * n_s
    at = ((col % 2) * n_x + col // 2) * n_s + s
    live = jnp.arange(cap, dtype=jnp.int32) < view_counts[0, 0][:, None]
    marks = jnp.where(live, view_rows[0, 0] + 1, 0)[:, None, :]
    own_list = jnp.arange(lists, dtype=jnp.int32)[None, :, None] == at
    meta = jnp.where(own_list, marks, 0).reshape(n_s, lists * cap)
    meta = jnp.pad(meta, ((0, 0), (0, -(lists * cap) % 128)))[:, None, :]

    dma = pltpu.SemaphoreType.DMA
    blocks = lambda n: (n, PK, 128)
    src, fwd_form, adj_form, gain, view_total, vector = call(
        functools.partial(start_kernel, n_x, n_s),
        [
            (blocks(rows), BF16),
            ((rows, tall, 128), BF16),
            ((rows, 128, tall), BF16),
            (blocks(size), F32),
            (blocks(size), F32),
            (blocks(3 * rows), BF16),
        ],
        [
            pltpu.VMEM(emission.shape, BF16),
            pltpu.VMEM(form.shape, BF16),
            pltpu.VMEM((lists, cap, BLK * CONF), BF16),
            pltpu.VMEM((lists,) + meta.shape[1:], jnp.int32),
            pltpu.VMEM((lists * cap, BLK * CONF), F32),
            pltpu.VMEM(blocks(size), F32),
        ]
        + [dma((2 * n_s + 12 * n_x,))] * 2 + [dma((4,))],
        (emission, view_grads[0, 0], form, reflect.reshape(-1, 128), meta, rows_perm, lanes_perm),
        hbm=3,
        vmem_bytes=FIRST_BYTES,
        remote=0,
    )
    group = n_x * size

    def forward(sources):
        return call(
            functools.partial(forward_local, slots),
            [(blocks(3 * rows), BF16)],
            [pltpu.VMEM(blocks(3 * rows), F32)],
            (index, fwd_form, sources),
            smem=1,
        )[0]

    bufs = [
        pltpu.VMEM(blocks(3 * group), BF16),
        pltpu.VMEM((2,) + blocks(group), BF16),
        pltpu.VMEM((2,) + blocks(group), BF16),
        pltpu.VMEM((n_x - 1,) + blocks(size), F32),
        pltpu.VMEM((n_x - 1,) + blocks(size), F32),
        pltpu.VMEM(blocks(rows), F32),
        pltpu.VMEM(blocks(group), F32),
        pltpu.VMEM((n_x - 1,) + blocks(size), F32),
        pltpu.VMEM((n_x - 1,) + blocks(size), F32),
    ]
    first_sums, bounced, adjoint_one, next_vector = call(
        functools.partial(middle_kernel, slots, n_x, n_s),
        [
            (blocks(size), F32),
            (blocks(rows), BF16),
            (blocks(size), F32),
            (blocks(3 * rows), BF16),
        ],
        bufs + [dma((16 * n_x,))] * 2,
        (index, forward(src), src, gain, vector, adj_form),
        smem=1,
        remote=1,
    )
    grad_emission, grad_reflect = call(
        functools.partial(end_kernel, slots, n_x, n_s),
        [((size, BLK * CONF), F32), ((size // 2, 128), F32)],
        bufs + [dma((8 * n_x,))] * 2,
        (index, forward(bounced), next_vector, adj_form, first_sums, adjoint_one, view_total),
        smem=1,
        remote=2,
    )
    return grad_emission, grad_reflect.reshape(size * BLK)


def solution(mesh):
    in_specs = (
        P(("level", "space", "col"), None),
        P(("level", "space", "col")),
        P(("level", "space"), "col", None, None),
        P(("level", "space"), "col", None),
        P(("level", "space"), "col", None, None, None),
        P(("level", "space"), "col", None, None),
        P(("level", "space"), "col", None),
    )
    out_specs = (P(("level", "space", "col"), None), P(("level", "space", "col")))
    step = functools.partial(body, mesh.shape["space"], mesh.shape["col"])
    return jax.shard_map(step, mesh=mesh, in_specs=in_specs, out_specs=out_specs, check_vma=False)
```
